256 devices in a mesh: dp: 32 (over x, z_hi, core), tensor: 8 (over y, z_lo).
Axes of the slice: x: 4, y: 4, z: 8 (z_hi: 4, z_lo: 2; z = z_hi * 2 + z_lo), core: 2. Of those that a mesh axis runs over, the one named last changes fastest.
Arguments:
- tokens: bfloat16 [64, 192, 4096], P('dp', None, 'tensor'), may hold values from -6 to 6
- grad_out: bfloat16 [64, 192, 4096], P('dp', None, 'tensor'), may hold values from -6 to 6
- counts: int32 [32], replicated, may hold values from 0 to 2, as said below
- gain: bfloat16 [4096], P('dp'), may hold values from 0.5 to 1.5
- wq: bfloat16 [4096, 4096], P('dp', 'tensor'), may hold values from -2.5 to 2.5
- wk: bfloat16 [4096, 1024], P('dp', 'tensor'), may hold values from -0.09375 to 0.09375
- wv: bfloat16 [4096, 1024], P('dp', 'tensor'), may hold values from -0.09375 to 0.09375
- wo: bfloat16 [4096, 4096], P('tensor', 'dp'), may hold values from -0.09375 to 0.09375
Outputs:
- mixed: bfloat16 [64, 192, 4096], P('dp', None, 'tensor')
- grad_tokens: bfloat16 [64, 192, 4096], P('dp', None, 'tensor')
- grad_gain: float32 [4096], P('dp')
- grad_wq: float32 [4096, 4096], P('dp', 'tensor')
- grad_wk: float32 [4096, 1024], P('dp', 'tensor')
- grad_wv: float32 [4096, 1024], P('dp', 'tensor')
- grad_wo: float32 [4096, 4096], P('tensor', 'dp')
The draws below stay inside these ranges and needn't reach their ends.
Inputs may be any that keep to these rules, and one draw needn't show every extreme that they name: `counts`: replica r and replica r + 16 hold 2 live blocks together; in every draw some replica holds 2.
All inputs are finite; a program needn't handle non-finite values.
Results may differ from the reference program's by a relative error of at most 0.025.
Values may be sent and summed in bfloat16 or wider, within the bound.
No kernel may reach another device: no remote copies, remote signals or barrier semaphores. Data moves between devices by JAX's collectives and lax.ppermute only.
A program may use at most 128 MiB of HBM per device.

```python
import jax
import jax.numpy as jnp
from jax import lax

D = 4096
HEADS = 32
KV = 8
HD = 128
BLK = 192
MAXB = 2
REPLICAS = 32
GROUPS = 8
SLOTS = 64


def draw_counts(key, part):
    half = REPLICAS // 2
    first_key = jax.random.fold_in(key, 41)
    pick_key = jax.random.fold_in(key, 42)
    side_key = jax.random.fold_in(key, 43)
    first = jax.random.randint(first_key, (half,), 0, 3)
    pick = jax.random.randint(pick_key, (), 0, half)
    corner = 2 * jax.random.randint(side_key, (), 0, 2)
    first = jnp.where(jnp.arange(half) == pick, corner, first)
    return jnp.concatenate([first, 2 - first]).astype(jnp.int32)


def key_matrix(key):
    sample = jax.random.truncated_normal(jax.random.fold_in(key, 31), -6.0, 6.0, (D, KV * HD), jnp.float32)
    return sample * D ** (-0.5)


def draw_wk(key, part):
    return key_matrix(key).astype(jnp.bfloat16)


def draw_wq(key, part):
    noise = jax.random.truncated_normal(jax.random.fold_in(key, 32), -6.0, 6.0, (D, HEADS * HD), jnp.float32)
    noise = noise * D ** (-0.5)
    return noise.astype(jnp.bfloat16)


def levels(own_key, extent, pieces, low, largest):
    level, own = 1.0, jax.random.fold_in(own_key, 6)
    for axis_at, shards_of in pieces:
        draws = jnp.exp(jax.random.uniform(jax.random.fold_in(own, axis_at), (shards_of,), jnp.float32, low / len(pieces), largest / len(pieces)))
        level = level * jnp.repeat(draws, extent[axis_at] // shards_of).reshape([-1 if axis == axis_at else 1 for axis in range(len(extent))])
    return level


def gaussian(own_key, shape, scale, reach, split=(), kind=jnp.bfloat16):
    result = scale * jax.random.normal(own_key, shape, jnp.float32)
    if split:
        result = result * levels(own_key, shape, split, -0.22, 0.18)
    return jnp.clip(result, -reach, reach).astype(kind)


def setup_inputs(seed: int = 0) -> dict:
    keys = jax.random.split(jax.random.key(seed), 9)
    return {
        "tokens": gaussian(keys[0], (SLOTS, BLK, D), 1.0, 6.0, ((0, 32), (2, 8))),
        "grad_out": gaussian(keys[1], (SLOTS, BLK, D), 1.0, 6.0, ((0, 32), (2, 8))),
        "counts": draw_counts(jax.random.fold_in(keys[8], 71), 0),
        "gain": jnp.clip(1.0 + 0.1 * jax.random.normal(keys[3], (D,), jnp.float32), 0.5, 1.5).astype(jnp.bfloat16),
        "wq": draw_wq(jax.random.fold_in(keys[8], 71), 0),
        "wk": draw_wk(jax.random.fold_in(keys[8], 71), 0),
        "wv": gaussian(keys[6], (D, KV * HD), D ** -0.5, 0.09375, ((0, 32), (1, 8))),
        "wo": gaussian(keys[7], (HEADS * HD, D), (HEADS * HD) ** -0.5, 0.09375, ((0, 8), (1, 32))),
    }


epsilon = 1e-05

def rounded(value):
    return lax.optimization_barrier(value.astype(jnp.bfloat16)).astype(jnp.float32)

def reference(tokens, grad_out, counts, gain, wq, wk, wv, wo):
    repeat = HEADS // KV
    query_cols = HEADS * HD // GROUPS
    key_cols = KV * HD // GROUPS
    score_scale = HD ** (-0.5)
    gain_float = gain.astype(jnp.float32)
    wq_float = wq.astype(jnp.float32)
    wk_float = wk.astype(jnp.float32)
    wv_float = wv.astype(jnp.float32)
    wo_float = wo.astype(jnp.float32)
    position = jnp.arange(BLK)
    causal = position[None, :] <= position[:, None]
    block_tokens = tokens.reshape(REPLICAS, MAXB, BLK, D)
    block_grads = grad_out.reshape(REPLICAS, MAXB, BLK, D)

    def replica_step(carry, inputs):
        block_in, block_grad, own_count = inputs
        live_mask = (jnp.arange(MAXB) < own_count).astype(jnp.float32)[:, None, None]
        wide_in = block_in.astype(jnp.float32)
        inverse_rms = lax.rsqrt(lax.optimization_barrier(jnp.mean(wide_in * wide_in, axis=-1, keepdims=True)) + epsilon)
        unit_rows = wide_in * inverse_rms
        normed = rounded(unit_rows * gain_float)
        queries = rounded(jnp.einsum('btd,dk->btk', normed, wq_float))
        key_rows = rounded(jnp.einsum('btd,dk->btk', normed, wk_float))
        values = rounded(jnp.einsum('btd,dk->btk', normed, wv_float))
        query_heads = queries.reshape(MAXB, BLK, KV, repeat, HD)
        key_heads = key_rows.reshape(MAXB, BLK, KV, HD)
        value_heads = values.reshape(MAXB, BLK, KV, HD)
        scores = jnp.einsum('btgrh,bugh->bgrtu', query_heads, key_heads) * score_scale
        scores = jnp.where(causal, scores, -1e+30)
        row_max = lax.optimization_barrier(jnp.max(scores, axis=-1, keepdims=True))
        exp_scores = jnp.exp(scores - row_max)
        softmax_out = exp_scores / lax.optimization_barrier(jnp.sum(exp_scores, axis=-1, keepdims=True))
        softmax_low = rounded(softmax_out)
        context = rounded(jnp.einsum('bgrtu,bugh->btgrh', softmax_low, value_heads))
        context = context.reshape(MAXB, BLK, HEADS * HD)
        head_terms = rounded(jnp.einsum('btgk,gkd->btgd', context.reshape(MAXB, BLK, GROUPS, query_cols), wo_float.reshape(GROUPS, query_cols, D)))
        attn_sum = lax.optimization_barrier(jnp.sum(head_terms, axis=2))
        mixed = ((wide_in + attn_sum) * live_mask).astype(jnp.bfloat16)
        upstream = block_grad.astype(jnp.float32) * live_mask
        grad_context = rounded(jnp.einsum('btd,kd->btk', upstream, wo_float)).reshape(MAXB, BLK, KV, repeat, HD)
        grad_soft = jnp.einsum('btgrh,bugh->bgrtu', grad_context, value_heads)
        row_inner = lax.optimization_barrier(jnp.sum(grad_soft * softmax_out, axis=-1, keepdims=True))
        grad_scores = rounded(softmax_out * (grad_soft - row_inner) * score_scale)
        grad_query = rounded(jnp.einsum('bgrtu,bugh->btgrh', grad_scores, key_heads)).reshape(MAXB, BLK, HEADS * HD)
        grad_key = rounded(jnp.einsum('bgrtu,btgrh->bugh', grad_scores, query_heads)).reshape(MAXB, BLK, KV * HD)
        grad_value = rounded(jnp.einsum('bgrtu,btgrh->bugh', softmax_low, grad_context)).reshape(MAXB, BLK, KV * HD)
        normed_terms = jnp.einsum('btgk,dgk->btgd', grad_query.reshape(MAXB, BLK, GROUPS, query_cols), wq_float.reshape(D, GROUPS, query_cols))
        normed_terms = normed_terms + jnp.einsum('btgk,dgk->btgd', grad_key.reshape(MAXB, BLK, GROUPS, key_cols), wk_float.reshape(D, GROUPS, key_cols))
        normed_terms = normed_terms + jnp.einsum('btgk,dgk->btgd', grad_value.reshape(MAXB, BLK, GROUPS, key_cols), wv_float.reshape(D, GROUPS, key_cols))
        grad_normed = lax.optimization_barrier(jnp.sum(rounded(normed_terms), axis=2))
        scaled = grad_normed * gain_float
        row_mean = lax.optimization_barrier(jnp.mean(scaled * unit_rows, axis=-1, keepdims=True))
        grad_tokens = (upstream + inverse_rms * (scaled - unit_rows * row_mean)).astype(jnp.bfloat16)
        carry = (carry[0] + rounded(lax.optimization_barrier(jnp.sum(grad_normed * unit_rows, axis=(0, 1)))), carry[1] + rounded(jnp.einsum('btd,btk->dk', normed, grad_query)), carry[2] + rounded(jnp.einsum('btd,btk->dk', normed, grad_key)), carry[3] + rounded(jnp.einsum('btd,btk->dk', normed, grad_value)), carry[4] + rounded(jnp.einsum('btk,btd->kd', context, upstream)))
        return (carry, (mixed, grad_tokens))
    start = (jnp.zeros((D,), jnp.float32), jnp.zeros((D, HEADS * HD), jnp.float32), jnp.zeros((D, KV * HD), jnp.float32), jnp.zeros((D, KV * HD), jnp.float32), jnp.zeros((HEADS * HD, D), jnp.float32))
    totals, outputs = lax.scan(replica_step, start, (block_tokens, block_grads, counts.astype(jnp.int32)))
    mixed = outputs[0].reshape(SLOTS, BLK, D)
    grad_tokens = outputs[1].reshape(SLOTS, BLK, D)
    return (mixed, grad_tokens, totals[0], totals[1], totals[2], totals[3], totals[4])
```

```python
import jax
import jax.numpy as jnp
from jax import lax
from jax.sharding import PartitionSpec as P

HEADS = 32
KV = 8
HD = 128


epsilon = 1e-05


def attention_forward(query_heads, key_heads, value_heads):
    length = query_heads.shape[1]
    score_scale = query_heads.shape[-1] ** (-0.5)
    position = jnp.arange(length)
    causal = position[None, :] <= position[:, None]
    scores = (
        jnp.einsum("btgrh,bugh->bgrtu", query_heads, key_heads, preferred_element_type=jnp.float32)
        * score_scale
    )
    scores = jnp.where(causal, scores, -1e30)
    row_max = jnp.max(scores, axis=-1, keepdims=True)
    exp_scores = jnp.exp(scores - row_max)
    softmax_out = exp_scores / jnp.sum(exp_scores, axis=-1, keepdims=True)
    softmax_low = softmax_out.astype(jnp.bfloat16)
    context = jnp.einsum(
        "bgrtu,bugh->btgrh", softmax_low, value_heads, preferred_element_type=jnp.float32
    ).astype(jnp.bfloat16)
    return (softmax_out, softmax_low, context)


def attention_backward(grad_context, query_heads, key_heads, value_heads, softmax_out, softmax_low):
    score_scale = query_heads.shape[-1] ** (-0.5)
    grad_soft = jnp.einsum(
        "btgrh,bugh->bgrtu", grad_context, value_heads, preferred_element_type=jnp.float32
    )
    row_inner = jnp.sum(grad_soft * softmax_out, axis=-1, keepdims=True)
    grad_scores = (softmax_out * (grad_soft - row_inner) * score_scale).astype(jnp.bfloat16)
    grad_query = jnp.einsum(
        "bgrtu,bugh->btgrh", grad_scores, key_heads, preferred_element_type=jnp.float32
    ).astype(jnp.bfloat16)
    grad_key = jnp.einsum(
        "bgrtu,btgrh->bugh", grad_scores, query_heads, preferred_element_type=jnp.float32
    ).astype(jnp.bfloat16)
    grad_value = jnp.einsum(
        "bgrtu,btgrh->bugh", softmax_low, grad_context, preferred_element_type=jnp.float32
    ).astype(jnp.bfloat16)
    return (grad_query, grad_key, grad_value)


def on_device(tokens, grad_out, counts, gain, wq, wk, wv, wo):
    groups = lax.axis_size("tensor")
    dp_size = lax.axis_size("dp")
    replica = lax.axis_index("dp")
    own_count = counts[replica]
    blocks, length, shard_width = tokens.shape
    full_width = shard_width * groups
    d_local = gain.shape[0]
    q_cols = wq.shape[1]
    k_cols = wk.shape[1]
    o_rows = wo.shape[0]
    lane = wo.shape[1]
    pack = jnp.concatenate(
        [
            jnp.pad(gain.reshape(1, d_local), ((0, 7), (0, 0))),
            wq.reshape(d_local * q_cols // lane, lane),
            wk.reshape(d_local * k_cols // lane, lane),
            wv.reshape(d_local * k_cols // lane, lane),
            wo,
        ],
        axis=0,
    )
    packed = lax.all_gather(pack, "dp", axis=0, tiled=False)
    r0 = 8
    r1 = r0 + d_local * q_cols // lane
    r2 = r1 + d_local * k_cols // lane
    r3 = r2 + d_local * k_cols // lane
    r4 = r3 + o_rows
    gain_all = packed[:, 0, :].reshape(full_width)
    wq_all = packed[:, r0:r1, :].reshape(dp_size * d_local, q_cols)
    wk_all = packed[:, r1:r2, :].reshape(dp_size * d_local, k_cols)
    wv_all = packed[:, r2:r3, :].reshape(dp_size * d_local, k_cols)
    wo_blk = packed[:, r3:r4, :]
    live_mask = (jnp.arange(blocks) < own_count).astype(jnp.bfloat16)[:, None, None]
    block_grad = grad_out * live_mask
    both = lax.all_gather(jnp.stack([tokens, block_grad]), "tensor", axis=3, tiled=True)
    wide_in, upstream = both[0], both[1]
    repeat = HEADS // KV
    kv_local = wk_all.shape[1] // HD
    wide_float = wide_in.astype(jnp.float32)
    inverse_rms = lax.rsqrt(jnp.mean(wide_float * wide_float, axis=-1, keepdims=True) + epsilon)
    unit_rows = wide_float * inverse_rms
    gain_float = gain_all.astype(jnp.float32)
    normed_float = unit_rows * gain_float
    normed = normed_float.astype(jnp.bfloat16)
    queries = jnp.einsum("btd,dk->btk", normed, wq_all, preferred_element_type=jnp.float32).astype(
        jnp.bfloat16
    )
    key_rows = jnp.einsum("btd,dk->btk", normed, wk_all, preferred_element_type=jnp.float32).astype(
        jnp.bfloat16
    )
    values = jnp.einsum("btd,dk->btk", normed, wv_all, preferred_element_type=jnp.float32).astype(
        jnp.bfloat16
    )
    query_heads = queries.reshape(blocks, length, kv_local, repeat, HD)
    key_heads = key_rows.reshape(blocks, length, kv_local, HD)
    value_heads = values.reshape(blocks, length, kv_local, HD)
    softmax_out, softmax_low, context = attention_forward(query_heads, key_heads, value_heads)
    context_flat = context.reshape(blocks, length, kv_local * repeat * HD)
    partial_value = jnp.einsum(
        "btk,jkl->btjl", context_flat, wo_blk, preferred_element_type=jnp.float32
    ).reshape(blocks, length, full_width)
    upstream_blk = upstream.reshape(blocks, length, dp_size, lane)
    grad_context = jnp.einsum(
        "btjl,jkl->btk", upstream_blk, wo_blk, preferred_element_type=jnp.float32
    ).astype(jnp.bfloat16)
    grad_output_proj = jnp.einsum(
        "btk,btjl->jkl", context_flat, upstream_blk, preferred_element_type=jnp.float32
    )
    grad_query, grad_key, grad_value = attention_backward(
        grad_context.reshape(blocks, length, kv_local, repeat, HD),
        query_heads,
        key_heads,
        value_heads,
        softmax_out,
        softmax_low,
    )
    grad_query = grad_query.reshape(blocks, length, -1)
    grad_key = grad_key.reshape(blocks, length, -1)
    grad_value = grad_value.reshape(blocks, length, -1)
    normed_terms = jnp.einsum("btk,dk->btd", grad_query, wq_all, preferred_element_type=jnp.float32)
    normed_terms = normed_terms + jnp.einsum(
        "btk,dk->btd", grad_key, wk_all, preferred_element_type=jnp.float32
    )
    normed_terms = normed_terms + jnp.einsum(
        "btk,dk->btd", grad_value, wv_all, preferred_element_type=jnp.float32
    )
    grad_query_proj = jnp.einsum(
        "btd,btk->dk", normed, grad_query, preferred_element_type=jnp.float32
    )
    grad_key_proj = jnp.einsum("btd,btk->dk", normed, grad_key, preferred_element_type=jnp.float32)
    grad_value_proj = jnp.einsum(
        "btd,btk->dk", normed, grad_value, preferred_element_type=jnp.float32
    )
    term_low = normed_terms.astype(jnp.bfloat16)
    term_float = term_low.astype(jnp.float32)
    rows = blocks * length
    row_dot = jnp.sum(term_float * normed_float, axis=-1).reshape(rows)
    gain_part = jnp.sum(term_float * unit_rows, axis=(0, 1))
    extra_rows = 1 + full_width // shard_width
    extra = jnp.concatenate(
        [
            jnp.pad(row_dot, (0, shard_width - rows)).reshape(1, shard_width),
            gain_part.reshape(full_width // shard_width, shard_width),
        ],
        axis=0,
    )
    extra_pad = (-extra_rows) % 8
    extra = jnp.pad(extra, ((0, extra_pad), (0, 0))).astype(jnp.bfloat16)

    def by_chunk(x):
        return x.reshape(rows, groups, shard_width).transpose(1, 0, 2)

    payload = jnp.concatenate(
        [
            by_chunk(partial_value.astype(jnp.bfloat16)),
            by_chunk(term_low),
            jnp.broadcast_to(extra[None], (groups,) + extra.shape),
        ],
        axis=1,
    )
    reduced = lax.psum_scatter(payload, "tensor", scatter_dimension=0, tiled=True)[0]
    reduced = reduced.astype(jnp.float32)
    attn_sum = reduced[:rows].reshape(blocks, length, shard_width)
    grad_normed = reduced[rows : 2 * rows].reshape(blocks, length, shard_width)
    row_mean = (reduced[2 * rows, :rows] / full_width).reshape(blocks, length, 1)
    gain_term = reduced[2 * rows + 1 : 2 * rows + extra_rows].reshape(full_width)
    mixed_block = ((tokens.astype(jnp.float32) + attn_sum) * live_mask.astype(jnp.float32)).astype(
        jnp.bfloat16
    )
    shard_start = lax.axis_index("tensor") * shard_width
    own_unit = lax.dynamic_slice_in_dim(unit_rows, shard_start, shard_width, 2)
    own_gain = lax.dynamic_slice_in_dim(gain_float, shard_start, shard_width, 0)
    own_grad = inverse_rms * (grad_normed * own_gain - own_unit * row_mean)
    grad_block = (block_grad.astype(jnp.float32) + own_grad).astype(jnp.bfloat16)
    gpack = jnp.concatenate(
        [
            jnp.pad(gain_term.reshape(dp_size, 1, d_local), ((0, 0), (0, 7), (0, 0))),
            grad_query_proj.reshape(dp_size, d_local * q_cols // lane, lane),
            grad_key_proj.reshape(dp_size, d_local * k_cols // lane, lane),
            grad_value_proj.reshape(dp_size, d_local * k_cols // lane, lane),
            grad_output_proj,
        ],
        axis=1,
    ).astype(jnp.bfloat16)
    greduced = lax.psum_scatter(gpack, "dp", scatter_dimension=0, tiled=True)[0].astype(jnp.float32)
    grad_gain = greduced[0]
    grad_wq = greduced[r0:r1].reshape(d_local, q_cols)
    grad_wk = greduced[r1:r2].reshape(d_local, k_cols)
    grad_wv = greduced[r2:r3].reshape(d_local, k_cols)
    grad_wo = greduced[r3:r4]
    return (mixed_block, grad_block, grad_gain, grad_wq, grad_wk, grad_wv, grad_wo)


def solution(mesh):
    return jax.shard_map(
        on_device,
        mesh=mesh,
        in_specs=(
            P("dp", None, "tensor"),
            P("dp", None, "tensor"),
            P(),
            P("dp"),
            P("dp", "tensor"),
            P("dp", "tensor"),
            P("dp", "tensor"),
            P("tensor", "dp"),
        ),
        out_specs=(
            P("dp", None, "tensor"),
            P("dp", None, "tensor"),
            P("dp"),
            P("dp", "tensor"),
            P("dp", "tensor"),
            P("dp", "tensor"),
            P("tensor", "dp"),
        ),
        check_vma=False,
    )
```

```python
import jax
import jax.numpy as jnp
from jax import lax
from jax.sharding import PartitionSpec as P

HEADS = 32
KV = 8
HD = 128


epsilon = 1e-05


def attention_forward(query_heads, key_heads, value_heads):
    length = query_heads.shape[1]
    score_scale = query_heads.shape[-1] ** (-0.5)
    position = jnp.arange(length)
    causal = position[None, :] <= position[:, None]
    scores = (
        jnp.einsum("btgrh,bugh->bgrtu", query_heads, key_heads, preferred_element_type=jnp.float32)
        * score_scale
    )
    scores = jnp.where(causal, scores, -1e30)
    row_max = jnp.max(scores, axis=-1, keepdims=True)
    exp_scores = jnp.exp(scores - row_max)
    softmax_out = exp_scores / jnp.sum(exp_scores, axis=-1, keepdims=True)
    softmax_low = softmax_out.astype(jnp.bfloat16)
    context = jnp.einsum(
        "bgrtu,bugh->btgrh", softmax_low, value_heads, preferred_element_type=jnp.float32
    ).astype(jnp.bfloat16)
    return (softmax_out, softmax_low, context)


def attention_backward(grad_context, query_heads, key_heads, value_heads, softmax_out, softmax_low):
    score_scale = query_heads.shape[-1] ** (-0.5)
    grad_soft = jnp.einsum(
        "btgrh,bugh->bgrtu", grad_context, value_heads, preferred_element_type=jnp.float32
    )
    row_inner = jnp.sum(grad_soft * softmax_out, axis=-1, keepdims=True)
    grad_scores = (softmax_out * (grad_soft - row_inner) * score_scale).astype(jnp.bfloat16)
    grad_query = jnp.einsum(
        "bgrtu,bugh->btgrh", grad_scores, key_heads, preferred_element_type=jnp.float32
    ).astype(jnp.bfloat16)
    grad_key = jnp.einsum(
        "bgrtu,btgrh->bugh", grad_scores, query_heads, preferred_element_type=jnp.float32
    ).astype(jnp.bfloat16)
    grad_value = jnp.einsum(
        "bgrtu,btgrh->bugh", softmax_low, grad_context, preferred_element_type=jnp.float32
    ).astype(jnp.bfloat16)
    return (grad_query, grad_key, grad_value)


def on_device(tokens, grad_out, counts, gain, wq, wk, wv, wo):
    groups = lax.axis_size("tensor")
    dp_size = lax.axis_size("dp")
    replica = lax.axis_index("dp")
    own_count = counts[replica]
    blocks, length, shard_width = tokens.shape
    full_width = shard_width * groups
    d_local = gain.shape[0]
    q_cols = wq.shape[1]
    k_cols = wk.shape[1]
    o_rows = wo.shape[0]
    lane = wo.shape[1]
    pack = jnp.concatenate(
        [
            jnp.pad(gain.reshape(1, d_local), ((0, 7), (0, 0))),
            wq.reshape(d_local * q_cols // lane, lane),
            wk.reshape(d_local * k_cols // lane, lane),
            wv.reshape(d_local * k_cols // lane, lane),
            wo,
        ],
        axis=0,
    )
    packed = lax.all_gather(pack, "dp", axis=0, tiled=False)
    r0 = 8
    r1 = r0 + d_local * q_cols // lane
    r2 = r1 + d_local * k_cols // lane
    r3 = r2 + d_local * k_cols // lane
    r4 = r3 + o_rows
    gain_all = packed[:, 0, :].reshape(full_width)
    wq_all = packed[:, r0:r1, :].reshape(dp_size * d_local, q_cols)
    wk_all = packed[:, r1:r2, :].reshape(dp_size * d_local, k_cols)
    wv_all = packed[:, r2:r3, :].reshape(dp_size * d_local, k_cols)
    wo_blk = packed[:, r3:r4, :]
    live_mask = (jnp.arange(blocks) < own_count).astype(jnp.bfloat16)[:, None, None]
    block_grad = grad_out * live_mask
    piece = jnp.stack([tokens, block_grad])
    spread = jnp.broadcast_to(piece[None], (groups,) + piece.shape)
    gathered = lax.all_to_all(spread, "tensor", 0, 0, tiled=True)
    both = jnp.moveaxis(gathered, 0, 3).reshape(2, blocks, length, full_width)
    wide_in, upstream = both[0], both[1]
    repeat = HEADS // KV
    kv_local = wk_all.shape[1] // HD
    wide_float = wide_in.astype(jnp.float32)
    inverse_rms = lax.rsqrt(jnp.mean(wide_float * wide_float, axis=-1, keepdims=True) + epsilon)
    unit_rows = wide_float * inverse_rms
    gain_float = gain_all.astype(jnp.float32)
    normed_float = unit_rows * gain_float
    normed = normed_float.astype(jnp.bfloat16)
    queries = jnp.einsum("btd,dk->btk", normed, wq_all, preferred_element_type=jnp.float32).astype(
        jnp.bfloat16
    )
    key_rows = jnp.einsum("btd,dk->btk", normed, wk_all, preferred_element_type=jnp.float32).astype(
        jnp.bfloat16
    )
    values = jnp.einsum("btd,dk->btk", normed, wv_all, preferred_element_type=jnp.float32).astype(
        jnp.bfloat16
    )
    query_heads = queries.reshape(blocks, length, kv_local, repeat, HD)
    key_heads = key_rows.reshape(blocks, length, kv_local, HD)
    value_heads = values.reshape(blocks, length, kv_local, HD)
    softmax_out, softmax_low, context = attention_forward(query_heads, key_heads, value_heads)
    context_flat = context.reshape(blocks, length, kv_local * repeat * HD)
    partial_value = jnp.einsum(
        "btk,jkl->btjl", context_flat, wo_blk, preferred_element_type=jnp.float32
    ).reshape(blocks, length, full_width)
    upstream_blk = upstream.reshape(blocks, length, dp_size, lane)
    grad_context = jnp.einsum(
        "btjl,jkl->btk", upstream_blk, wo_blk, preferred_element_type=jnp.float32
    ).astype(jnp.bfloat16)
    grad_output_proj = jnp.einsum(
        "btk,btjl->jkl", context_flat, upstream_blk, preferred_element_type=jnp.float32
    )
    grad_query, grad_key, grad_value = attention_backward(
        grad_context.reshape(blocks, length, kv_local, repeat, HD),
        query_heads,
        key_heads,
        value_heads,
        softmax_out,
        softmax_low,
    )
    grad_query = grad_query.reshape(blocks, length, -1)
    grad_key = grad_key.reshape(blocks, length, -1)
    grad_value = grad_value.reshape(blocks, length, -1)
    normed_terms = jnp.einsum("btk,dk->btd", grad_query, wq_all, preferred_element_type=jnp.float32)
    normed_terms = normed_terms + jnp.einsum(
        "btk,dk->btd", grad_key, wk_all, preferred_element_type=jnp.float32
    )
    normed_terms = normed_terms + jnp.einsum(
        "btk,dk->btd", grad_value, wv_all, preferred_element_type=jnp.float32
    )
    grad_query_proj = jnp.einsum(
        "btd,btk->dk", normed, grad_query, preferred_element_type=jnp.float32
    )
    grad_key_proj = jnp.einsum("btd,btk->dk", normed, grad_key, preferred_element_type=jnp.float32)
    grad_value_proj = jnp.einsum(
        "btd,btk->dk", normed, grad_value, preferred_element_type=jnp.float32
    )
    term_low = normed_terms.astype(jnp.bfloat16)
    term_float = term_low.astype(jnp.float32)
    rows = blocks * length
    row_dot = jnp.sum(term_float * normed_float, axis=-1).reshape(rows)
    gain_part = jnp.sum(term_float * unit_rows, axis=(0, 1))
    extra = jnp.pad(row_dot, (0, shard_width - rows)).reshape(1, shard_width)
    extra = jnp.pad(extra, ((0, 7), (0, 0))).astype(jnp.bfloat16)

    def by_chunk(x):
        return x.reshape(rows, groups, shard_width).transpose(1, 0, 2)

    payload = jnp.concatenate(
        [
            by_chunk(partial_value.astype(jnp.bfloat16)),
            by_chunk(term_low),
            jnp.broadcast_to(extra[None], (groups,) + extra.shape),
        ],
        axis=1,
    )
    received = lax.all_to_all(payload, "tensor", 0, 0, tiled=True)
    reduced = jnp.sum(received.astype(jnp.float32), axis=0)
    attn_sum = reduced[:rows].reshape(blocks, length, shard_width)
    grad_normed = reduced[rows : 2 * rows].reshape(blocks, length, shard_width)
    row_mean = (reduced[2 * rows, :rows] / full_width).reshape(blocks, length, 1)
    mixed_block = ((tokens.astype(jnp.float32) + attn_sum) * live_mask.astype(jnp.float32)).astype(
        jnp.bfloat16
    )
    shard_start = lax.axis_index("tensor") * shard_width
    own_unit = lax.dynamic_slice_in_dim(unit_rows, shard_start, shard_width, 2)
    own_gain = lax.dynamic_slice_in_dim(gain_float, shard_start, shard_width, 0)
    own_grad = inverse_rms * (grad_normed * own_gain - own_unit * row_mean)
    grad_block = (block_grad.astype(jnp.float32) + own_grad).astype(jnp.bfloat16)
    gpack = jnp.concatenate(
        [
            jnp.pad(gain_part.reshape(dp_size, 1, d_local), ((0, 0), (0, 7), (0, 0))),
            grad_query_proj.reshape(dp_size, d_local * q_cols // lane, lane),
            grad_key_proj.reshape(dp_size, d_local * k_cols // lane, lane),
            grad_value_proj.reshape(dp_size, d_local * k_cols // lane, lane),
            grad_output_proj,
        ],
        axis=1,
    ).astype(jnp.bfloat16)
    greduced = lax.psum_scatter(gpack, "dp", scatter_dimension=0, tiled=True)[0].astype(jnp.float32)
    gain_spread = jnp.broadcast_to(greduced[0][None], (groups, d_local))
    grad_gain = jnp.sum(lax.all_to_all(gain_spread, "tensor", 0, 0, tiled=True), axis=0)
    grad_wq = greduced[r0:r1].reshape(d_local, q_cols)
    grad_wk = greduced[r1:r2].reshape(d_local, k_cols)
    grad_wv = greduced[r2:r3].reshape(d_local, k_cols)
    grad_wo = greduced[r3:r4]
    return (mixed_block, grad_block, grad_gain, grad_wq, grad_wk, grad_wv, grad_wo)


def solution(mesh):
    return jax.shard_map(
        on_device,
        mesh=mesh,
        in_specs=(
            P("dp", None, "tensor"),
            P("dp", None, "tensor"),
            P(),
            P("dp"),
            P("dp", "tensor"),
            P("dp", "tensor"),
            P("dp", "tensor"),
            P("tensor", "dp"),
        ),
        out_specs=(
            P("dp", None, "tensor"),
            P("dp", None, "tensor"),
            P("dp"),
            P("dp", "tensor"),
            P("dp", "tensor"),
            P("dp", "tensor"),
            P("tensor", "dp"),
        ),
        check_vma=False,
    )
```

```python
import jax
import jax.numpy as jnp
from jax import lax
from jax.sharding import PartitionSpec as P

HEADS = 32
KV = 8
HD = 128


epsilon = 1e-05


def attention_forward(query_heads, key_heads, value_heads):
    length = query_heads.shape[1]
    score_scale = query_heads.shape[-1] ** (-0.5)
    position = jnp.arange(length)
    causal = position[None, :] <= position[:, None]
    scores = (
        jnp.einsum("btgrh,bugh->bgrtu", query_heads, key_heads, preferred_element_type=jnp.float32)
        * score_scale
    )
    scores = jnp.where(causal, scores, -1e30)
    row_max = jnp.max(scores, axis=-1, keepdims=True)
    exp_scores = jnp.exp(scores - row_max)
    softmax_out = exp_scores / jnp.sum(exp_scores, axis=-1, keepdims=True)
    softmax_low = softmax_out.astype(jnp.bfloat16)
    context = jnp.einsum(
        "bgrtu,bugh->btgrh", softmax_low, value_heads, preferred_element_type=jnp.float32
    ).astype(jnp.bfloat16)
    return (softmax_out, softmax_low, context)


def attention_backward(grad_context, query_heads, key_heads, value_heads, softmax_out, softmax_low):
    score_scale = query_heads.shape[-1] ** (-0.5)
    grad_soft = jnp.einsum(
        "btgrh,bugh->bgrtu", grad_context, value_heads, preferred_element_type=jnp.float32
    )
    row_inner = jnp.sum(grad_soft * softmax_out, axis=-1, keepdims=True)
    grad_scores = (softmax_out * (grad_soft - row_inner) * score_scale).astype(jnp.bfloat16)
    grad_query = jnp.einsum(
        "bgrtu,bugh->btgrh", grad_scores, key_heads, preferred_element_type=jnp.float32
    ).astype(jnp.bfloat16)
    grad_key = jnp.einsum(
        "bgrtu,btgrh->bugh", grad_scores, query_heads, preferred_element_type=jnp.float32
    ).astype(jnp.bfloat16)
    grad_value = jnp.einsum(
        "bgrtu,btgrh->bugh", softmax_low, grad_context, preferred_element_type=jnp.float32
    ).astype(jnp.bfloat16)
    return (grad_query, grad_key, grad_value)


def on_device(tokens, grad_out, counts, gain, wq, wk, wv, wo):
    groups = lax.axis_size("tensor")
    dp_size = lax.axis_size("dp")
    replica = lax.axis_index("dp")
    own_count = counts[replica]
    blocks, length, shard_width = tokens.shape
    full_width = shard_width * groups
    d_local = gain.shape[0]
    q_cols = wq.shape[1]
    k_cols = wk.shape[1]
    o_rows = wo.shape[0]
    lane = wo.shape[1]
    pack = jnp.concatenate(
        [
            jnp.pad(gain.reshape(1, d_local), ((0, 7), (0, 0))),
            wq.reshape(d_local * q_cols // lane, lane),
            wk.reshape(d_local * k_cols // lane, lane),
            wv.reshape(d_local * k_cols // lane, lane),
            wo,
        ],
        axis=0,
    )
    packed = lax.all_gather(pack, "dp", axis=0, tiled=False)
    r0 = 8
    r1 = r0 + d_local * q_cols // lane
    r2 = r1 + d_local * k_cols // lane
    r3 = r2 + d_local * k_cols // lane
    r4 = r3 + o_rows
    gain_all = packed[:, 0, :].reshape(full_width)
    wq_all = packed[:, r0:r1, :].reshape(dp_size * d_local, q_cols)
    wk_all = packed[:, r1:r2, :].reshape(dp_size * d_local, k_cols)
    wv_all = packed[:, r2:r3, :].reshape(dp_size * d_local, k_cols)
    wo_blk = packed[:, r3:r4, :]
    half = dp_size // 2
    pair = [(i, (i + half) % dp_size) for i in range(dp_size)]
    partner_count = counts[(replica + half) % dp_size]
    lent = lax.ppermute(jnp.stack([tokens[1], grad_out[1]]), "dp", pair)
    borrow = own_count == 0
    work_live = jnp.where(borrow, partner_count >= 2, own_count >= 1)
    live_mask = work_live.astype(jnp.bfloat16)
    work_tokens = jnp.where(borrow, lent[0], tokens[0])[None]
    block_grad = (jnp.where(borrow, lent[1], grad_out[0]) * live_mask)[None]
    full_blocks = blocks
    blocks = 1
    piece = jnp.stack([work_tokens, block_grad])
    spread = jnp.broadcast_to(piece[None], (groups,) + piece.shape)
    gathered = lax.all_to_all(spread, "tensor", 0, 0, tiled=True)
    both = jnp.moveaxis(gathered, 0, 3).reshape(2, blocks, length, full_width)
    wide_in, upstream = both[0], both[1]
    repeat = HEADS // KV
    kv_local = wk_all.shape[1] // HD
    wide_float = wide_in.astype(jnp.float32)
    inverse_rms = lax.rsqrt(jnp.mean(wide_float * wide_float, axis=-1, keepdims=True) + epsilon)
    unit_rows = wide_float * inverse_rms
    gain_float = gain_all.astype(jnp.float32)
    normed_float = unit_rows * gain_float
    normed = normed_float.astype(jnp.bfloat16)
    queries = jnp.einsum("btd,dk->btk", normed, wq_all, preferred_element_type=jnp.float32).astype(
        jnp.bfloat16
    )
    key_rows = jnp.einsum("btd,dk->btk", normed, wk_all, preferred_element_type=jnp.float32).astype(
        jnp.bfloat16
    )
    values = jnp.einsum("btd,dk->btk", normed, wv_all, preferred_element_type=jnp.float32).astype(
        jnp.bfloat16
    )
    query_heads = queries.reshape(blocks, length, kv_local, repeat, HD)
    key_heads = key_rows.reshape(blocks, length, kv_local, HD)
    value_heads = values.reshape(blocks, length, kv_local, HD)
    softmax_out, softmax_low, context = attention_forward(query_heads, key_heads, value_heads)
    context_flat = context.reshape(blocks, length, kv_local * repeat * HD)
    partial_value = jnp.einsum(
        "btk,jkl->btjl", context_flat, wo_blk, preferred_element_type=jnp.float32
    ).reshape(blocks, length, full_width)
    upstream_blk = upstream.reshape(blocks, length, dp_size, lane)
    grad_context = jnp.einsum(
        "btjl,jkl->btk", upstream_blk, wo_blk, preferred_element_type=jnp.float32
    ).astype(jnp.bfloat16)
    grad_output_proj = jnp.einsum(
        "btk,btjl->jkl", context_flat, upstream_blk, preferred_element_type=jnp.float32
    )
    grad_query, grad_key, grad_value = attention_backward(
        grad_context.reshape(blocks, length, kv_local, repeat, HD),
        query_heads,
        key_heads,
        value_heads,
        softmax_out,
        softmax_low,
    )
    grad_query = grad_query.reshape(blocks, length, -1)
    grad_key = grad_key.reshape(blocks, length, -1)
    grad_value = grad_value.reshape(blocks, length, -1)
    normed_terms = jnp.einsum("btk,dk->btd", grad_query, wq_all, preferred_element_type=jnp.float32)
    normed_terms = normed_terms + jnp.einsum(
        "btk,dk->btd", grad_key, wk_all, preferred_element_type=jnp.float32
    )
    normed_terms = normed_terms + jnp.einsum(
        "btk,dk->btd", grad_value, wv_all, preferred_element_type=jnp.float32
    )
    grad_query_proj = jnp.einsum(
        "btd,btk->dk", normed, grad_query, preferred_element_type=jnp.float32
    )
    grad_key_proj = jnp.einsum("btd,btk->dk", normed, grad_key, preferred_element_type=jnp.float32)
    grad_value_proj = jnp.einsum(
        "btd,btk->dk", normed, grad_value, preferred_element_type=jnp.float32
    )
    term_low = normed_terms.astype(jnp.bfloat16)
    term_float = term_low.astype(jnp.float32)
    rows = blocks * length
    row_dot = jnp.sum(term_float * normed_float, axis=-1).reshape(rows)
    gain_part = jnp.sum(term_float * unit_rows, axis=(0, 1))
    extra = jnp.pad(row_dot, (0, shard_width - rows)).reshape(1, shard_width)
    extra = jnp.pad(extra, ((0, 7), (0, 0))).astype(jnp.bfloat16)

    def by_chunk(x):
        return x.reshape(rows, groups, shard_width).transpose(1, 0, 2)

    payload = jnp.concatenate(
        [
            by_chunk(partial_value.astype(jnp.bfloat16)),
            by_chunk(term_low),
            jnp.broadcast_to(extra[None], (groups,) + extra.shape),
        ],
        axis=1,
    )
    received = lax.all_to_all(payload, "tensor", 0, 0, tiled=True)
    reduced = jnp.sum(received.astype(jnp.float32), axis=0)
    attn_sum = reduced[:rows].reshape(blocks, length, shard_width)
    grad_normed = reduced[rows : 2 * rows].reshape(blocks, length, shard_width)
    row_mean = (reduced[2 * rows, :rows] / full_width).reshape(blocks, length, 1)
    mixed_block = ((work_tokens.astype(jnp.float32) + attn_sum) * live_mask.astype(jnp.float32)).astype(
        jnp.bfloat16
    )
    shard_start = lax.axis_index("tensor") * shard_width
    own_unit = lax.dynamic_slice_in_dim(unit_rows, shard_start, shard_width, 2)
    own_gain = lax.dynamic_slice_in_dim(gain_float, shard_start, shard_width, 0)
    own_grad = inverse_rms * (grad_normed * own_gain - own_unit * row_mean)
    grad_block = (block_grad.astype(jnp.float32) + own_grad).astype(jnp.bfloat16)
    work_out = jnp.stack([mixed_block[0], grad_block[0]])
    returned = lax.ppermute(work_out, "dp", pair)
    first = jnp.where(own_count >= 1, work_out, jnp.zeros_like(work_out))
    second = jnp.where(own_count >= 2, returned, jnp.zeros_like(returned))
    mixed_block = jnp.stack([first[0], second[0]])
    grad_block = jnp.stack([first[1], second[1]])
    gpack = jnp.concatenate(
        [
            jnp.pad(gain_part.reshape(dp_size, 1, d_local), ((0, 0), (0, 7), (0, 0))),
            grad_query_proj.reshape(dp_size, d_local * q_cols // lane, lane),
            grad_key_proj.reshape(dp_size, d_local * k_cols // lane, lane),
            grad_value_proj.reshape(dp_size, d_local * k_cols // lane, lane),
            grad_output_proj,
        ],
        axis=1,
    ).astype(jnp.bfloat16)
    greduced = lax.psum_scatter(gpack, "dp", scatter_dimension=0, tiled=True)[0].astype(jnp.float32)
    gain_spread = jnp.broadcast_to(greduced[0][None], (groups, d_local))
    grad_gain = jnp.sum(lax.all_to_all(gain_spread, "tensor", 0, 0, tiled=True), axis=0)
    grad_wq = greduced[r0:r1].reshape(d_local, q_cols)
    grad_wk = greduced[r1:r2].reshape(d_local, k_cols)
    grad_wv = greduced[r2:r3].reshape(d_local, k_cols)
    grad_wo = greduced[r3:r4]
    return (mixed_block, grad_block, grad_gain, grad_wq, grad_wk, grad_wv, grad_wo)


def solution(mesh):
    return jax.shard_map(
        on_device,
        mesh=mesh,
        in_specs=(
            P("dp", None, "tensor"),
            P("dp", None, "tensor"),
            P(),
            P("dp"),
            P("dp", "tensor"),
            P("dp", "tensor"),
            P("dp", "tensor"),
            P("tensor", "dp"),
        ),
        out_specs=(
            P("dp", None, "tensor"),
            P("dp", None, "tensor"),
            P("dp"),
            P("dp", "tensor"),
            P("dp", "tensor"),
            P("dp", "tensor"),
            P("tensor", "dp"),
        ),
        check_vma=False,
    )
```

```python
import jax
import jax.numpy as jnp
from jax import lax
from jax.sharding import PartitionSpec as P

HEADS = 32
KV = 8
HD = 128


epsilon = 1e-05


def attention_forward(query_heads, key_heads, value_heads):
    length = query_heads.shape[1]
    score_scale = query_heads.shape[-1] ** (-0.5)
    position = jnp.arange(length)
    causal = position[None, :] <= position[:, None]
    scores = (
        jnp.einsum("btgrh,bugh->bgrtu", query_heads, key_heads, preferred_element_type=jnp.float32)
        * score_scale
    )
    scores = jnp.where(causal, scores, -1e30)
    row_max = jnp.max(scores, axis=-1, keepdims=True)
    exp_scores = jnp.exp(scores - row_max)
    softmax_out = exp_scores / jnp.sum(exp_scores, axis=-1, keepdims=True)
    softmax_low = softmax_out.astype(jnp.bfloat16)
    context = jnp.einsum(
        "bgrtu,bugh->btgrh", softmax_low, value_heads, preferred_element_type=jnp.float32
    ).astype(jnp.bfloat16)
    return (softmax_out, softmax_low, context)


def attention_backward(grad_context, query_heads, key_heads, value_heads, softmax_out, softmax_low):
    score_scale = query_heads.shape[-1] ** (-0.5)
    grad_soft = jnp.einsum(
        "btgrh,bugh->bgrtu", grad_context, value_heads, preferred_element_type=jnp.float32
    )
    row_inner = jnp.sum(grad_soft * softmax_out, axis=-1, keepdims=True)
    grad_scores = (softmax_out * (grad_soft - row_inner) * score_scale).astype(jnp.bfloat16)
    grad_query = jnp.einsum(
        "bgrtu,bugh->btgrh", grad_scores, key_heads, preferred_element_type=jnp.float32
    ).astype(jnp.bfloat16)
    grad_key = jnp.einsum(
        "bgrtu,btgrh->bugh", grad_scores, query_heads, preferred_element_type=jnp.float32
    ).astype(jnp.bfloat16)
    grad_value = jnp.einsum(
        "bgrtu,btgrh->bugh", softmax_low, grad_context, preferred_element_type=jnp.float32
    ).astype(jnp.bfloat16)
    return (grad_query, grad_key, grad_value)


def on_device(tokens, grad_out, counts, gain, wq, wk, wv, wo):
    groups = lax.axis_size("tensor")
    dp_size = lax.axis_size("dp")
    replica = lax.axis_index("dp")
    own_count = counts[replica]
    blocks, length, shard_width = tokens.shape
    full_width = shard_width * groups
    d_local = gain.shape[0]
    q_cols = wq.shape[1]
    k_cols = wk.shape[1]
    o_rows = wo.shape[0]
    lane = wo.shape[1]
    pack = jnp.concatenate(
        [
            jnp.pad(gain.reshape(1, d_local), ((0, 15), (0, 0))),
            wq.reshape(d_local * q_cols // lane, lane),
            wk.reshape(d_local * k_cols // lane, lane),
            wv.reshape(d_local * k_cols // lane, lane),
            wo,
        ],
        axis=0,
    )
    packed = lax.all_gather(pack, "dp", axis=0, tiled=False)
    r0 = 16
    r1 = r0 + d_local * q_cols // lane
    r2 = r1 + d_local * k_cols // lane
    r3 = r2 + d_local * k_cols // lane
    r4 = r3 + o_rows
    gain_all = packed[:, 0, :].reshape(full_width)
    wq_all = packed[:, r0:r1, :].reshape(dp_size * d_local, q_cols)
    wk_all = packed[:, r1:r2, :].reshape(dp_size * d_local, k_cols)
    wv_all = packed[:, r2:r3, :].reshape(dp_size * d_local, k_cols)
    wo_blk = packed[:, r3:r4, :]
    half = dp_size // 2
    pair = [(i, (i + half) % dp_size) for i in range(dp_size)]
    partner_count = counts[(replica + half) % dp_size]
    lent = lax.ppermute(jnp.stack([tokens[1], grad_out[1]]), "dp", pair)
    borrow = own_count == 0
    work_live = jnp.where(borrow, partner_count >= 2, own_count >= 1)
    live_mask = work_live.astype(jnp.bfloat16)
    work_tokens = jnp.where(borrow, lent[0], tokens[0])[None]
    block_grad = (jnp.where(borrow, lent[1], grad_out[0]) * live_mask)[None]
    full_blocks = blocks
    blocks = 1
    piece = jnp.stack([work_tokens, block_grad])
    spread = jnp.broadcast_to(piece[None], (groups,) + piece.shape)
    gathered = lax.all_to_all(spread, "tensor", 0, 0, tiled=True)
    both = jnp.moveaxis(gathered, 0, 3).reshape(2, blocks, length, full_width)
    wide_in, upstream = both[0], both[1]
    repeat = HEADS // KV
    kv_local = wk_all.shape[1] // HD
    wide_float = wide_in.astype(jnp.float32)
    inverse_rms = lax.rsqrt(jnp.mean(wide_float * wide_float, axis=-1, keepdims=True) + epsilon)
    unit_rows = wide_float * inverse_rms
    gain_float = gain_all.astype(jnp.float32)
    normed_float = unit_rows * gain_float
    normed = normed_float.astype(jnp.bfloat16)
    queries = jnp.einsum("btd,dk->btk", normed, wq_all, preferred_element_type=jnp.float32).astype(
        jnp.bfloat16
    )
    key_rows = jnp.einsum("btd,dk->btk", normed, wk_all, preferred_element_type=jnp.float32).astype(
        jnp.bfloat16
    )
    values = jnp.einsum("btd,dk->btk", normed, wv_all, preferred_element_type=jnp.float32).astype(
        jnp.bfloat16
    )
    query_heads = queries.reshape(blocks, length, kv_local, repeat, HD)
    key_heads = key_rows.reshape(blocks, length, kv_local, HD)
    value_heads = values.reshape(blocks, length, kv_local, HD)
    softmax_out, softmax_low, context = attention_forward(query_heads, key_heads, value_heads)
    context_flat = context.reshape(blocks, length, kv_local * repeat * HD)
    partial_value = jnp.einsum(
        "btk,jkl->btjl", context_flat, wo_blk, preferred_element_type=jnp.float32
    ).reshape(blocks, length, full_width)
    upstream_blk = upstream.reshape(blocks, length, dp_size, lane)
    grad_context = jnp.einsum(
        "btjl,jkl->btk", upstream_blk, wo_blk, preferred_element_type=jnp.float32
    ).astype(jnp.bfloat16)
    grad_output_proj = jnp.einsum(
        "btk,btjl->jkl", context_flat, upstream_blk, preferred_element_type=jnp.float32
    )
    grad_query, grad_key, grad_value = attention_backward(
        grad_context.reshape(blocks, length, kv_local, repeat, HD),
        query_heads,
        key_heads,
        value_heads,
        softmax_out,
        softmax_low,
    )
    grad_query = grad_query.reshape(blocks, length, -1)
    grad_key = grad_key.reshape(blocks, length, -1)
    grad_value = grad_value.reshape(blocks, length, -1)
    normed_terms = jnp.einsum("btk,dk->btd", grad_query, wq_all, preferred_element_type=jnp.float32)
    normed_terms = normed_terms + jnp.einsum(
        "btk,dk->btd", grad_key, wk_all, preferred_element_type=jnp.float32
    )
    normed_terms = normed_terms + jnp.einsum(
        "btk,dk->btd", grad_value, wv_all, preferred_element_type=jnp.float32
    )
    grad_query_proj = jnp.einsum(
        "btd,btk->dk", normed, grad_query, preferred_element_type=jnp.float32
    )
    grad_key_proj = jnp.einsum("btd,btk->dk", normed, grad_key, preferred_element_type=jnp.float32)
    grad_value_proj = jnp.einsum(
        "btd,btk->dk", normed, grad_value, preferred_element_type=jnp.float32
    )
    term_low = normed_terms.astype(jnp.bfloat16)
    term_float = term_low.astype(jnp.float32)
    rows = blocks * length
    row_dot = jnp.sum(term_float * normed_float, axis=-1).reshape(rows)
    gain_part = jnp.sum(term_float * unit_rows, axis=(0, 1))
    extra = jnp.pad(row_dot, (0, shard_width - rows)).reshape(1, shard_width)
    extra = jnp.pad(extra, ((0, 15), (0, 0))).astype(jnp.bfloat16)

    def by_chunk(x):
        return x.reshape(rows, groups, shard_width).transpose(1, 0, 2)

    payload = jnp.concatenate(
        [
            by_chunk(partial_value.astype(jnp.bfloat16)),
            by_chunk(term_low),
            jnp.broadcast_to(extra[None], (groups,) + extra.shape),
        ],
        axis=1,
    )
    received = lax.all_to_all(payload, "tensor", 0, 0, tiled=True)
    reduced = jnp.sum(received.astype(jnp.float32), axis=0)
    attn_sum = reduced[:rows].reshape(blocks, length, shard_width)
    grad_normed = reduced[rows : 2 * rows].reshape(blocks, length, shard_width)
    row_mean = (reduced[2 * rows, :rows] / full_width).reshape(blocks, length, 1)
    mixed_block = ((work_tokens.astype(jnp.float32) + attn_sum) * live_mask.astype(jnp.float32)).astype(
        jnp.bfloat16
    )
    shard_start = lax.axis_index("tensor") * shard_width
    own_unit = lax.dynamic_slice_in_dim(unit_rows, shard_start, shard_width, 2)
    own_gain = lax.dynamic_slice_in_dim(gain_float, shard_start, shard_width, 0)
    own_grad = inverse_rms * (grad_normed * own_gain - own_unit * row_mean)
    grad_block = (block_grad.astype(jnp.float32) + own_grad).astype(jnp.bfloat16)
    work_out = jnp.stack([mixed_block[0], grad_block[0]])
    returned = lax.ppermute(work_out, "dp", pair)
    first = jnp.where(own_count >= 1, work_out, jnp.zeros_like(work_out))
    second = jnp.where(own_count >= 2, returned, jnp.zeros_like(returned))
    mixed_block = jnp.stack([first[0], second[0]])
    grad_block = jnp.stack([first[1], second[1]])
    gpack = jnp.concatenate(
        [
            jnp.pad(gain_part.reshape(dp_size, 1, d_local), ((0, 0), (0, 15), (0, 0))),
            grad_query_proj.reshape(dp_size, d_local * q_cols // lane, lane),
            grad_key_proj.reshape(dp_size, d_local * k_cols // lane, lane),
            grad_value_proj.reshape(dp_size, d_local * k_cols // lane, lane),
            grad_output_proj,
        ],
        axis=1,
    ).astype(jnp.bfloat16)
    greduced = lax.psum_scatter(gpack, "dp", scatter_dimension=0, tiled=True)[0].astype(jnp.float32)
    gain_spread = jnp.broadcast_to(greduced[0][None], (groups, d_local))
    grad_gain = jnp.sum(lax.all_to_all(gain_spread, "tensor", 0, 0, tiled=True), axis=0)
    grad_wq = greduced[r0:r1].reshape(d_local, q_cols)
    grad_wk = greduced[r1:r2].reshape(d_local, k_cols)
    grad_wv = greduced[r2:r3].reshape(d_local, k_cols)
    grad_wo = greduced[r3:r4]
    return (mixed_block, grad_block, grad_gain, grad_wq, grad_wk, grad_wv, grad_wo)


def solution(mesh):
    return jax.shard_map(
        on_device,
        mesh=mesh,
        in_specs=(
            P("dp", None, "tensor"),
            P("dp", None, "tensor"),
            P(),
            P("dp"),
            P("dp", "tensor"),
            P("dp", "tensor"),
            P("dp", "tensor"),
            P("tensor", "dp"),
        ),
        out_specs=(
            P("dp", None, "tensor"),
            P("dp", None, "tensor"),
            P("dp"),
            P("dp", "tensor"),
            P("dp", "tensor"),
            P("dp", "tensor"),
            P("tensor", "dp"),
        ),
        check_vma=False,
    )
```

```python
import jax
import jax.numpy as jnp
from jax import lax
from jax.sharding import Mesh, PartitionSpec as P

HEADS = 32
KV = 8
HD = 128


epsilon = 1e-05


def attention_forward(query_heads, key_heads, value_heads):
    length = query_heads.shape[1]
    score_scale = query_heads.shape[-1] ** (-0.5)
    position = jnp.arange(length)
    causal = position[None, :] <= position[:, None]
    scores = (
        jnp.einsum("btgrh,bugh->bgrtu", query_heads, key_heads, preferred_element_type=jnp.float32)
        * score_scale
    )
    scores = jnp.where(causal, scores, -1e30)
    row_max = jnp.max(scores, axis=-1, keepdims=True)
    exp_scores = jnp.exp(scores - row_max)
    softmax_out = exp_scores / jnp.sum(exp_scores, axis=-1, keepdims=True)
    softmax_low = softmax_out.astype(jnp.bfloat16)
    context = jnp.einsum(
        "bgrtu,bugh->btgrh", softmax_low, value_heads, preferred_element_type=jnp.float32
    ).astype(jnp.bfloat16)
    return (softmax_out, softmax_low, context)


def attention_backward(grad_context, query_heads, key_heads, value_heads, softmax_out, softmax_low):
    score_scale = query_heads.shape[-1] ** (-0.5)
    grad_soft = jnp.einsum(
        "btgrh,bugh->bgrtu", grad_context, value_heads, preferred_element_type=jnp.float32
    )
    row_inner = jnp.sum(grad_soft * softmax_out, axis=-1, keepdims=True)
    grad_scores = (softmax_out * (grad_soft - row_inner) * score_scale).astype(jnp.bfloat16)
    grad_query = jnp.einsum(
        "bgrtu,bugh->btgrh", grad_scores, key_heads, preferred_element_type=jnp.float32
    ).astype(jnp.bfloat16)
    grad_key = jnp.einsum(
        "bgrtu,btgrh->bugh", grad_scores, query_heads, preferred_element_type=jnp.float32
    ).astype(jnp.bfloat16)
    grad_value = jnp.einsum(
        "bgrtu,btgrh->bugh", softmax_low, grad_context, preferred_element_type=jnp.float32
    ).astype(jnp.bfloat16)
    return (grad_query, grad_key, grad_value)


def on_device(tokens, grad_out, counts, gain, wq, wk, wv, wo):
    groups = lax.axis_size("tensor")
    dp_size = lax.axis_size("dq") * lax.axis_size("dc")
    replica = lax.axis_index(("dq", "dc"))
    own_count = counts[replica]
    blocks, length, shard_width = tokens.shape
    full_width = shard_width * groups
    d_local = gain.shape[0]
    q_cols = wq.shape[1]
    k_cols = wk.shape[1]
    o_rows = wo.shape[0]
    lane = wo.shape[1]
    pack = jnp.concatenate(
        [
            jnp.pad(gain.reshape(1, d_local), ((0, 15), (0, 0))),
            wq.reshape(d_local * q_cols // lane, lane),
            wk.reshape(d_local * k_cols // lane, lane),
            wv.reshape(d_local * k_cols // lane, lane),
            wo,
        ],
        axis=0,
    )
    half_gather = lax.all_gather(pack, "dq", axis=0, tiled=False)
    other_half = lax.ppermute(half_gather, "dc", [(0, 1), (1, 0)])
    core = lax.axis_index("dc")
    lower = jnp.where(core == 0, half_gather, other_half)
    upper = jnp.where(core == 0, other_half, half_gather)
    packed = jnp.stack([lower, upper], axis=1).reshape((dp_size,) + pack.shape)
    r0 = 16
    r1 = r0 + d_local * q_cols // lane
    r2 = r1 + d_local * k_cols // lane
    r3 = r2 + d_local * k_cols // lane
    r4 = r3 + o_rows
    gain_all = packed[:, 0, :].reshape(full_width)
    wq_all = packed[:, r0:r1, :].reshape(dp_size * d_local, q_cols)
    wk_all = packed[:, r1:r2, :].reshape(dp_size * d_local, k_cols)
    wv_all = packed[:, r2:r3, :].reshape(dp_size * d_local, k_cols)
    wo_blk = packed[:, r3:r4, :]
    half = dp_size // 2
    pair = [(i, (i + half) % dp_size) for i in range(dp_size)]
    partner_count = counts[(replica + half) % dp_size]
    lent = lax.ppermute(jnp.stack([tokens[1], grad_out[1]]), ("dq", "dc"), pair)
    borrow = own_count == 0
    work_live = jnp.where(borrow, partner_count >= 2, own_count >= 1)
    live_mask = work_live.astype(jnp.bfloat16)
    work_tokens = jnp.where(borrow, lent[0], tokens[0])[None]
    block_grad = (jnp.where(borrow, lent[1], grad_out[0]) * live_mask)[None]
    full_blocks = blocks
    blocks = 1
    piece = jnp.stack([work_tokens, block_grad])
    spread = jnp.broadcast_to(piece[None], (groups,) + piece.shape)
    gathered = lax.all_to_all(spread, "tensor", 0, 0, tiled=True)
    both = jnp.moveaxis(gathered, 0, 3).reshape(2, blocks, length, full_width)
    wide_in, upstream = both[0], both[1]
    repeat = HEADS // KV
    kv_local = wk_all.shape[1] // HD
    wide_float = wide_in.astype(jnp.float32)
    inverse_rms = lax.rsqrt(jnp.mean(wide_float * wide_float, axis=-1, keepdims=True) + epsilon)
    unit_rows = wide_float * inverse_rms
    gain_float = gain_all.astype(jnp.float32)
    normed_float = unit_rows * gain_float
    normed = normed_float.astype(jnp.bfloat16)
    queries = jnp.einsum("btd,dk->btk", normed, wq_all, preferred_element_type=jnp.float32).astype(
        jnp.bfloat16
    )
    key_rows = jnp.einsum("btd,dk->btk", normed, wk_all, preferred_element_type=jnp.float32).astype(
        jnp.bfloat16
    )
    values = jnp.einsum("btd,dk->btk", normed, wv_all, preferred_element_type=jnp.float32).astype(
        jnp.bfloat16
    )
    query_heads = queries.reshape(blocks, length, kv_local, repeat, HD)
    key_heads = key_rows.reshape(blocks, length, kv_local, HD)
    value_heads = values.reshape(blocks, length, kv_local, HD)
    softmax_out, softmax_low, context = attention_forward(query_heads, key_heads, value_heads)
    context_flat = context.reshape(blocks, length, kv_local * repeat * HD)
    partial_value = jnp.einsum(
        "btk,jkl->btjl", context_flat, wo_blk, preferred_element_type=jnp.float32
    ).reshape(blocks, length, full_width)
    upstream_blk = upstream.reshape(blocks, length, dp_size, lane)
    grad_context = jnp.einsum(
        "btjl,jkl->btk", upstream_blk, wo_blk, preferred_element_type=jnp.float32
    ).astype(jnp.bfloat16)
    grad_output_proj = jnp.einsum(
        "btk,btjl->jkl", context_flat, upstream_blk, preferred_element_type=jnp.float32
    )
    grad_query, grad_key, grad_value = attention_backward(
        grad_context.reshape(blocks, length, kv_local, repeat, HD),
        query_heads,
        key_heads,
        value_heads,
        softmax_out,
        softmax_low,
    )
    grad_query = grad_query.reshape(blocks, length, -1)
    grad_key = grad_key.reshape(blocks, length, -1)
    grad_value = grad_value.reshape(blocks, length, -1)
    normed_terms = jnp.einsum("btk,dk->btd", grad_query, wq_all, preferred_element_type=jnp.float32)
    normed_terms = normed_terms + jnp.einsum(
        "btk,dk->btd", grad_key, wk_all, preferred_element_type=jnp.float32
    )
    normed_terms = normed_terms + jnp.einsum(
        "btk,dk->btd", grad_value, wv_all, preferred_element_type=jnp.float32
    )
    grad_query_proj = jnp.einsum(
        "btd,btk->dk", normed, grad_query, preferred_element_type=jnp.float32
    )
    grad_key_proj = jnp.einsum("btd,btk->dk", normed, grad_key, preferred_element_type=jnp.float32)
    grad_value_proj = jnp.einsum(
        "btd,btk->dk", normed, grad_value, preferred_element_type=jnp.float32
    )
    term_low = normed_terms.astype(jnp.bfloat16)
    term_float = term_low.astype(jnp.float32)
    rows = blocks * length
    row_dot = jnp.sum(term_float * normed_float, axis=-1).reshape(rows)
    gain_part = jnp.sum(term_float * unit_rows, axis=(0, 1))
    extra = jnp.pad(row_dot, (0, shard_width - rows)).reshape(1, shard_width)
    extra = jnp.pad(extra, ((0, 15), (0, 0))).astype(jnp.bfloat16)

    def by_chunk(x):
        return x.reshape(rows, groups, shard_width).transpose(1, 0, 2)

    payload = jnp.concatenate(
        [
            by_chunk(partial_value.astype(jnp.bfloat16)),
            by_chunk(term_low),
            jnp.broadcast_to(extra[None], (groups,) + extra.shape),
        ],
        axis=1,
    )
    received = lax.all_to_all(payload, "tensor", 0, 0, tiled=True)
    reduced = jnp.sum(received.astype(jnp.float32), axis=0)
    attn_sum = reduced[:rows].reshape(blocks, length, shard_width)
    grad_normed = reduced[rows : 2 * rows].reshape(blocks, length, shard_width)
    row_mean = (reduced[2 * rows, :rows] / full_width).reshape(blocks, length, 1)
    mixed_block = ((work_tokens.astype(jnp.float32) + attn_sum) * live_mask.astype(jnp.float32)).astype(
        jnp.bfloat16
    )
    shard_start = lax.axis_index("tensor") * shard_width
    own_unit = lax.dynamic_slice_in_dim(unit_rows, shard_start, shard_width, 2)
    own_gain = lax.dynamic_slice_in_dim(gain_float, shard_start, shard_width, 0)
    own_grad = inverse_rms * (grad_normed * own_gain - own_unit * row_mean)
    grad_block = (block_grad.astype(jnp.float32) + own_grad).astype(jnp.bfloat16)
    work_out = jnp.stack([mixed_block[0], grad_block[0]])
    returned = lax.ppermute(work_out, ("dq", "dc"), pair)
    first = jnp.where(own_count >= 1, work_out, jnp.zeros_like(work_out))
    second = jnp.where(own_count >= 2, returned, jnp.zeros_like(returned))
    mixed_block = jnp.stack([first[0], second[0]])
    grad_block = jnp.stack([first[1], second[1]])
    gpack = jnp.concatenate(
        [
            jnp.pad(gain_part.reshape(dp_size, 1, d_local), ((0, 0), (0, 15), (0, 0))),
            grad_query_proj.reshape(dp_size, d_local * q_cols // lane, lane),
            grad_key_proj.reshape(dp_size, d_local * k_cols // lane, lane),
            grad_value_proj.reshape(dp_size, d_local * k_cols // lane, lane),
            grad_output_proj,
        ],
        axis=1,
    ).astype(jnp.bfloat16)
    by_core = gpack.reshape((dp_size // 2, 2) + gpack.shape[1:])
    core = lax.axis_index("dc")
    keep = lax.dynamic_index_in_dim(by_core, core, 1, keepdims=False)
    give = lax.dynamic_index_in_dim(by_core, 1 - core, 1, keepdims=False)
    got = lax.ppermute(give, "dc", [(0, 1), (1, 0)])
    pair_sum = (keep.astype(jnp.float32) + got.astype(jnp.float32)).astype(jnp.bfloat16)
    greduced = lax.psum_scatter(pair_sum, "dq", scatter_dimension=0, tiled=True)[0].astype(jnp.float32)
    gain_spread = jnp.broadcast_to(greduced[0][None], (groups, d_local))
    grad_gain = jnp.sum(lax.all_to_all(gain_spread, "tensor", 0, 0, tiled=True), axis=0)
    grad_wq = greduced[r0:r1].reshape(d_local, q_cols)
    grad_wk = greduced[r1:r2].reshape(d_local, k_cols)
    grad_wv = greduced[r2:r3].reshape(d_local, k_cols)
    grad_wo = greduced[r3:r4]
    return (mixed_block, grad_block, grad_gain, grad_wq, grad_wk, grad_wv, grad_wo)


def solution(mesh):
    split = Mesh(
        mesh.devices.reshape(mesh.shape["dp"] // 2, 2, mesh.shape["tensor"]), ("dq", "dc", "tensor")
    )
    return jax.shard_map(
        on_device,
        mesh=split,
        in_specs=(
            P(("dq", "dc"), None, "tensor"),
            P(("dq", "dc"), None, "tensor"),
            P(),
            P(("dq", "dc")),
            P(("dq", "dc"), "tensor"),
            P(("dq", "dc"), "tensor"),
            P(("dq", "dc"), "tensor"),
            P("tensor", ("dq", "dc")),
        ),
        out_specs=(
            P(("dq", "dc"), None, "tensor"),
            P(("dq", "dc"), None, "tensor"),
            P(("dq", "dc")),
            P(("dq", "dc"), "tensor"),
            P(("dq", "dc"), "tensor"),
            P(("dq", "dc"), "tensor"),
            P("tensor", ("dq", "dc")),
        ),
        check_vma=False,
    )
```

```python
import jax
import jax.numpy as jnp
from jax import lax
from jax.sharding import PartitionSpec as P

HEADS = 32
KV = 8
HD = 128


epsilon = 1e-05


def attention_forward(query_heads, key_heads, value_heads):
    length = query_heads.shape[1]
    score_scale = query_heads.shape[-1] ** (-0.5)
    position = jnp.arange(length)
    causal = position[None, :] <= position[:, None]
    scores = (
        jnp.einsum("btgrh,bugh->bgrtu", query_heads, key_heads, preferred_element_type=jnp.float32)
        * score_scale
    )
    scores = jnp.where(causal, scores, -1e30)
    row_max = jnp.max(scores, axis=-1, keepdims=True)
    exp_scores = jnp.exp(scores - row_max)
    softmax_out = exp_scores / jnp.sum(exp_scores, axis=-1, keepdims=True)
    softmax_low = softmax_out.astype(jnp.bfloat16)
    context = jnp.einsum(
        "bgrtu,bugh->btgrh", softmax_low, value_heads, preferred_element_type=jnp.float32
    ).astype(jnp.bfloat16)
    return (softmax_out, softmax_low, context)


def attention_backward(grad_context, query_heads, key_heads, value_heads, softmax_out, softmax_low):
    score_scale = query_heads.shape[-1] ** (-0.5)
    grad_soft = jnp.einsum(
        "btgrh,bugh->bgrtu", grad_context, value_heads, preferred_element_type=jnp.float32
    )
    row_inner = jnp.sum(grad_soft * softmax_out, axis=-1, keepdims=True)
    grad_scores = (softmax_out * (grad_soft - row_inner) * score_scale).astype(jnp.bfloat16)
    grad_query = jnp.einsum(
        "bgrtu,bugh->btgrh", grad_scores, key_heads, preferred_element_type=jnp.float32
    ).astype(jnp.bfloat16)
    grad_key = jnp.einsum(
        "bgrtu,btgrh->bugh", grad_scores, query_heads, preferred_element_type=jnp.float32
    ).astype(jnp.bfloat16)
    grad_value = jnp.einsum(
        "bgrtu,btgrh->bugh", softmax_low, grad_context, preferred_element_type=jnp.float32
    ).astype(jnp.bfloat16)
    return (grad_query, grad_key, grad_value)


def on_device(tokens, grad_out, counts, gain, wq, wk, wv, wo):
    groups = lax.axis_size("tensor")
    dp_size = lax.axis_size("dp")
    replica = lax.axis_index("dp")
    own_count = counts[replica]
    blocks, length, shard_width = tokens.shape
    full_width = shard_width * groups
    d_local = gain.shape[0]
    q_cols = wq.shape[1]
    k_cols = wk.shape[1]
    o_rows = wo.shape[0]
    c1 = q_cols
    c2 = c1 + k_cols
    c3 = c2 + k_cols
    c4 = c3 + o_rows
    pack = jnp.concatenate(
        [wq, wk, wv, wo.T, jnp.pad(gain.reshape(d_local, 1), ((0, 0), (0, 127)))], axis=1
    )
    packed = lax.all_gather(pack, "dp", axis=0, tiled=False)
    w_qkv = packed[:, :, :c3].reshape(dp_size * d_local, c3)
    wo_blk = packed[:, :, c3:c4]
    gain_all = packed[:, :, c4].reshape(full_width)
    half = dp_size // 2
    pair = [(i, (i + half) % dp_size) for i in range(dp_size)]
    partner_count = counts[(replica + half) % dp_size]
    lent = lax.ppermute(jnp.stack([tokens[1], grad_out[1]]), "dp", pair)
    borrow = own_count == 0
    work_live = jnp.where(borrow, partner_count >= 2, own_count >= 1)
    live_mask = work_live.astype(jnp.bfloat16)
    work_tokens = jnp.where(borrow, lent[0], tokens[0])
    work_grad = jnp.where(borrow, lent[1], grad_out[0]) * live_mask
    piece = jnp.stack([work_tokens, work_grad])
    spread = jnp.broadcast_to(piece[None], (groups,) + piece.shape)
    gathered = lax.all_to_all(spread, "tensor", 0, 0, tiled=True)
    both = jnp.moveaxis(gathered, 0, 2).reshape(2, length, full_width)
    wide_in, upstream = both[0], both[1]
    repeat = HEADS // KV
    kv_local = k_cols // HD
    wide_float = wide_in.astype(jnp.float32)
    inverse_rms = lax.rsqrt(jnp.mean(wide_float * wide_float, axis=-1, keepdims=True) + epsilon)
    unit_rows = wide_float * inverse_rms
    gain_float = gain_all.astype(jnp.float32)
    normed_float = unit_rows * gain_float
    normed = normed_float.astype(jnp.bfloat16)
    qkv = jnp.einsum("td,dk->tk", normed, w_qkv, preferred_element_type=jnp.float32).astype(
        jnp.bfloat16
    )
    query_heads = qkv[:, :c1].reshape(1, length, kv_local, repeat, HD)
    key_heads = qkv[:, c1:c2].reshape(1, length, kv_local, HD)
    value_heads = qkv[:, c2:c3].reshape(1, length, kv_local, HD)
    softmax_out, softmax_low, context = attention_forward(query_heads, key_heads, value_heads)
    context_flat = context.reshape(length, kv_local * repeat * HD)
    partial_value = jnp.einsum(
        "tk,jlk->tjl", context_flat, wo_blk, preferred_element_type=jnp.float32
    ).reshape(length, full_width)
    upstream_blk = upstream.reshape(length, dp_size, d_local)
    grad_context = jnp.einsum(
        "tjl,jlk->tk", upstream_blk, wo_blk, preferred_element_type=jnp.float32
    ).astype(jnp.bfloat16)
    grad_query, grad_key, grad_value = attention_backward(
        grad_context.reshape(1, length, kv_local, repeat, HD),
        query_heads,
        key_heads,
        value_heads,
        softmax_out,
        softmax_low,
    )
    grad_qkv = jnp.concatenate(
        [
            grad_query.reshape(length, c1),
            grad_key.reshape(length, k_cols),
            grad_value.reshape(length, k_cols),
        ],
        axis=1,
    )
    normed_terms = jnp.einsum("tk,dk->td", grad_qkv, w_qkv, preferred_element_type=jnp.float32)
    grad_w_qkv = jnp.einsum(
        "tjl,tk->jlk", normed.reshape(length, dp_size, d_local), grad_qkv,
        preferred_element_type=jnp.float32,
    )
    grad_output_t = jnp.einsum(
        "tjl,tk->jlk", upstream_blk, context_flat, preferred_element_type=jnp.float32
    )
    term_low = normed_terms.astype(jnp.bfloat16)
    term_float = term_low.astype(jnp.float32)
    row_dot = jnp.sum(term_float * normed_float, axis=-1)
    gain_part = jnp.sum(term_float * unit_rows, axis=0)
    extra = jnp.pad(row_dot, (0, shard_width - length)).reshape(1, shard_width)
    extra = jnp.pad(extra, ((0, 15), (0, 0))).astype(jnp.bfloat16)

    def by_chunk(x):
        return x.reshape(length, groups, shard_width).transpose(1, 0, 2)

    payload = jnp.concatenate(
        [
            by_chunk(partial_value.astype(jnp.bfloat16)),
            by_chunk(term_low),
            jnp.broadcast_to(extra[None], (groups,) + extra.shape),
        ],
        axis=1,
    )
    received = lax.all_to_all(payload, "tensor", 0, 0, tiled=True)
    reduced = jnp.sum(received.astype(jnp.float32), axis=0)
    attn_sum = reduced[:length]
    grad_normed = reduced[length : 2 * length]
    row_mean = (reduced[2 * length, :length] / full_width)[:, None]
    work_mixed = ((work_tokens.astype(jnp.float32) + attn_sum) * live_mask.astype(jnp.float32)).astype(
        jnp.bfloat16
    )
    shard_start = lax.axis_index("tensor") * shard_width
    own_unit = lax.dynamic_slice_in_dim(unit_rows, shard_start, shard_width, 1)
    own_gain = lax.dynamic_slice_in_dim(gain_float, shard_start, shard_width, 0)
    own_grad = inverse_rms * (grad_normed * own_gain - own_unit * row_mean)
    work_grad_tokens = (work_grad.astype(jnp.float32) + own_grad).astype(jnp.bfloat16)
    work_out = jnp.stack([work_mixed, work_grad_tokens])
    returned = lax.ppermute(work_out, "dp", pair)
    first = jnp.where(own_count >= 1, work_out, jnp.zeros_like(work_out))
    second = jnp.where(own_count >= 2, returned, jnp.zeros_like(returned))
    mixed_block = jnp.stack([first[0], second[0]])
    grad_block = jnp.stack([first[1], second[1]])
    gpack = jnp.concatenate(
        [
            grad_w_qkv.astype(jnp.bfloat16),
            grad_output_t.astype(jnp.bfloat16),
            jnp.pad(gain_part.reshape(dp_size, d_local, 1), ((0, 0), (0, 0), (0, 127))).astype(
                jnp.bfloat16
            ),
        ],
        axis=2,
    )
    greduced = lax.psum_scatter(gpack, "dp", scatter_dimension=0, tiled=True)[0].astype(jnp.float32)
    grad_wq = greduced[:, :c1]
    grad_wk = greduced[:, c1:c2]
    grad_wv = greduced[:, c2:c3]
    grad_wo = greduced[:, c3:c4].T
    gain_spread = jnp.broadcast_to(greduced[:, c4][None], (groups, d_local))
    grad_gain = jnp.sum(lax.all_to_all(gain_spread, "tensor", 0, 0, tiled=True), axis=0)
    return (mixed_block, grad_block, grad_gain, grad_wq, grad_wk, grad_wv, grad_wo)


def solution(mesh):
    return jax.shard_map(
        on_device,
        mesh=mesh,
        in_specs=(
            P("dp", None, "tensor"),
            P("dp", None, "tensor"),
            P(),
            P("dp"),
            P("dp", "tensor"),
            P("dp", "tensor"),
            P("dp", "tensor"),
            P("tensor", "dp"),
        ),
        out_specs=(
            P("dp", None, "tensor"),
            P("dp", None, "tensor"),
            P("dp"),
            P("dp", "tensor"),
            P("dp", "tensor"),
            P("dp", "tensor"),
            P("tensor", "dp"),
        ),
        check_vma=False,
    )
```

```python
import jax
import jax.numpy as jnp
from jax import lax
from jax.sharding import PartitionSpec as P

HEADS = 32
KV = 8
HD = 128


epsilon = 1e-05


def attention_forward(query_heads, key_heads, value_heads):
    length = query_heads.shape[1]
    score_scale = query_heads.shape[-1] ** (-0.5)
    position = jnp.arange(length)
    causal = position[None, :] <= position[:, None]
    scores = (
        jnp.einsum("btgrh,bugh->bgrtu", query_heads, key_heads, preferred_element_type=jnp.float32)
        * score_scale
    )
    scores = jnp.where(causal, scores, -1e30)
    row_max = jnp.max(scores, axis=-1, keepdims=True)
    exp_scores = jnp.exp(scores - row_max)
    softmax_out = exp_scores / jnp.sum(exp_scores, axis=-1, keepdims=True)
    softmax_low = softmax_out.astype(jnp.bfloat16)
    context = jnp.einsum(
        "bgrtu,bugh->btgrh", softmax_low, value_heads, preferred_element_type=jnp.float32
    ).astype(jnp.bfloat16)
    return (softmax_out, softmax_low, context)


def attention_backward(grad_context, query_heads, key_heads, value_heads, softmax_out, softmax_low):
    score_scale = query_heads.shape[-1] ** (-0.5)
    grad_soft = jnp.einsum(
        "btgrh,bugh->bgrtu", grad_context, value_heads, preferred_element_type=jnp.float32
    )
    row_inner = jnp.sum(grad_soft * softmax_out, axis=-1, keepdims=True)
    grad_scores = (softmax_out * (grad_soft - row_inner) * score_scale).astype(jnp.bfloat16)
    grad_query = jnp.einsum(
        "bgrtu,bugh->btgrh", grad_scores, key_heads, preferred_element_type=jnp.float32
    ).astype(jnp.bfloat16)
    grad_key = jnp.einsum(
        "bgrtu,btgrh->bugh", grad_scores, query_heads, preferred_element_type=jnp.float32
    ).astype(jnp.bfloat16)
    grad_value = jnp.einsum(
        "bgrtu,btgrh->bugh", softmax_low, grad_context, preferred_element_type=jnp.float32
    ).astype(jnp.bfloat16)
    return (grad_query, grad_key, grad_value)


def on_device(tokens, grad_out, counts, gain, wq, wk, wv, wo):
    groups = lax.axis_size("tensor")
    dp_size = lax.axis_size("dp")
    replica = lax.axis_index("dp")
    own_count = counts[replica]
    blocks, length, shard_width = tokens.shape
    full_width = shard_width * groups
    d_local = gain.shape[0]
    q_cols = wq.shape[1]
    k_cols = wk.shape[1]
    o_rows = wo.shape[0]
    c1 = q_cols
    c2 = c1 + k_cols
    c3 = c2 + k_cols
    c4 = c3 + o_rows
    pack = jnp.concatenate(
        [wq, wk, wv, wo.T, jnp.pad(gain.reshape(d_local, 1), ((0, 0), (0, 127)))], axis=1
    )
    packed = lax.all_gather(pack, "dp", axis=0, tiled=True)
    width = packed.shape[1]
    gain_all = packed[:, c4]
    half = dp_size // 2
    pair = [(i, (i + half) % dp_size) for i in range(dp_size)]
    partner_count = counts[(replica + half) % dp_size]
    lent = lax.ppermute(jnp.stack([tokens[1], grad_out[1]]), "dp", pair)
    borrow = own_count == 0
    work_live = jnp.where(borrow, partner_count >= 2, own_count >= 1)
    live_mask = work_live.astype(jnp.bfloat16)
    work_tokens = jnp.where(borrow, lent[0], tokens[0])
    work_grad = jnp.where(borrow, lent[1], grad_out[0]) * live_mask
    piece = jnp.stack([work_tokens, work_grad])
    spread = jnp.broadcast_to(piece[None], (groups,) + piece.shape)
    gathered = lax.all_to_all(spread, "tensor", 0, 0, tiled=True)
    both = jnp.moveaxis(gathered, 0, 2).reshape(2, length, full_width)
    wide_in, upstream = both[0], both[1]
    repeat = HEADS // KV
    kv_local = k_cols // HD
    wide_float = wide_in.astype(jnp.float32)
    inverse_rms = lax.rsqrt(jnp.mean(wide_float * wide_float, axis=-1, keepdims=True) + epsilon)
    unit_rows = wide_float * inverse_rms
    gain_float = gain_all.astype(jnp.float32)
    normed_float = unit_rows * gain_float
    normed = normed_float.astype(jnp.bfloat16)
    qkv = jnp.einsum("td,dk->tk", normed, packed, preferred_element_type=jnp.float32).astype(
        jnp.bfloat16
    )
    query_heads = qkv[:, :c1].reshape(1, length, kv_local, repeat, HD)
    key_heads = qkv[:, c1:c2].reshape(1, length, kv_local, HD)
    value_heads = qkv[:, c2:c3].reshape(1, length, kv_local, HD)
    softmax_out, softmax_low, context = attention_forward(query_heads, key_heads, value_heads)
    context_flat = context.reshape(length, kv_local * repeat * HD)
    context_wide = jnp.pad(context_flat, ((0, 0), (c3, width - c4)))
    partial_value = jnp.einsum(
        "tk,dk->td", context_wide, packed, preferred_element_type=jnp.float32
    )
    upstream_blk = upstream.reshape(length, dp_size, d_local)
    grad_context = jnp.einsum(
        "td,dk->tk", upstream, packed, preferred_element_type=jnp.float32
    )[:, c3:c4].astype(jnp.bfloat16)
    grad_query, grad_key, grad_value = attention_backward(
        grad_context.reshape(1, length, kv_local, repeat, HD),
        query_heads,
        key_heads,
        value_heads,
        softmax_out,
        softmax_low,
    )
    grad_qkv = jnp.concatenate(
        [
            grad_query.reshape(length, c1),
            grad_key.reshape(length, k_cols),
            grad_value.reshape(length, k_cols),
        ],
        axis=1,
    )
    grad_wide = jnp.pad(grad_qkv, ((0, 0), (0, width - c3)))
    normed_terms = jnp.einsum("tk,dk->td", grad_wide, packed, preferred_element_type=jnp.float32)
    grad_w_qkv = jnp.einsum(
        "tjl,tk->jlk", normed.reshape(length, dp_size, d_local), grad_qkv,
        preferred_element_type=jnp.float32,
    )
    grad_output_t = jnp.einsum(
        "tjl,tk->jlk", upstream_blk, context_flat, preferred_element_type=jnp.float32
    )
    term_low = normed_terms.astype(jnp.bfloat16)
    term_float = term_low.astype(jnp.float32)
    row_dot = jnp.sum(term_float * normed_float, axis=-1)
    gain_part = jnp.sum(term_float * unit_rows, axis=0)
    extra = jnp.pad(row_dot, (0, shard_width - length)).reshape(1, shard_width)
    extra = jnp.pad(extra, ((0, 15), (0, 0))).astype(jnp.bfloat16)

    def by_chunk(x):
        return x.reshape(length, groups, shard_width).transpose(1, 0, 2)

    payload = jnp.concatenate(
        [
            by_chunk(partial_value.astype(jnp.bfloat16)),
            by_chunk(term_low),
            jnp.broadcast_to(extra[None], (groups,) + extra.shape),
        ],
        axis=1,
    )
    received = lax.all_to_all(payload, "tensor", 0, 0, tiled=True)
    reduced = jnp.sum(received.astype(jnp.float32), axis=0)
    attn_sum = reduced[:length]
    grad_normed = reduced[length : 2 * length]
    row_mean = (reduced[2 * length, :length] / full_width)[:, None]
    work_mixed = ((work_tokens.astype(jnp.float32) + attn_sum) * live_mask.astype(jnp.float32)).astype(
        jnp.bfloat16
    )
    shard_start = lax.axis_index("tensor") * shard_width
    own_unit = lax.dynamic_slice_in_dim(unit_rows, shard_start, shard_width, 1)
    own_gain = lax.dynamic_slice_in_dim(gain_float, shard_start, shard_width, 0)
    own_grad = inverse_rms * (grad_normed * own_gain - own_unit * row_mean)
    work_grad_tokens = (work_grad.astype(jnp.float32) + own_grad).astype(jnp.bfloat16)
    work_out = jnp.stack([work_mixed, work_grad_tokens])
    returned = lax.ppermute(work_out, "dp", pair)
    first = jnp.where(own_count >= 1, work_out, jnp.zeros_like(work_out))
    second = jnp.where(own_count >= 2, returned, jnp.zeros_like(returned))
    mixed_block = jnp.stack([first[0], second[0]])
    grad_block = jnp.stack([first[1], second[1]])
    gpack = jnp.concatenate(
        [
            grad_w_qkv.astype(jnp.bfloat16),
            grad_output_t.astype(jnp.bfloat16),
            jnp.pad(gain_part.reshape(dp_size, d_local, 1), ((0, 0), (0, 0), (0, 127))).astype(
                jnp.bfloat16
            ),
        ],
        axis=2,
    )
    greduced = lax.psum_scatter(gpack, "dp", scatter_dimension=0, tiled=True)[0].astype(jnp.float32)
    grad_wq = greduced[:, :c1]
    grad_wk = greduced[:, c1:c2]
    grad_wv = greduced[:, c2:c3]
    grad_wo = greduced[:, c3:c4].T
    gain_spread = jnp.broadcast_to(greduced[:, c4][None], (groups, d_local))
    grad_gain = jnp.sum(lax.all_to_all(gain_spread, "tensor", 0, 0, tiled=True), axis=0)
    return (mixed_block, grad_block, grad_gain, grad_wq, grad_wk, grad_wv, grad_wo)


def solution(mesh):
    return jax.shard_map(
        on_device,
        mesh=mesh,
        in_specs=(
            P("dp", None, "tensor"),
            P("dp", None, "tensor"),
            P(),
            P("dp"),
            P("dp", "tensor"),
            P("dp", "tensor"),
            P("dp", "tensor"),
            P("tensor", "dp"),
        ),
        out_specs=(
            P("dp", None, "tensor"),
            P("dp", None, "tensor"),
            P("dp"),
            P("dp", "tensor"),
            P("dp", "tensor"),
            P("dp", "tensor"),
            P("tensor", "dp"),
        ),
        check_vma=False,
    )
```

```python
import jax
import jax.numpy as jnp
from jax import lax
from jax.sharding import PartitionSpec as P

HEADS = 32
KV = 8
HD = 128


epsilon = 1e-05


def attention_forward(query_heads, key_heads, value_heads):
    length = query_heads.shape[1]
    score_scale = query_heads.shape[-1] ** (-0.5)
    position = jnp.arange(length)
    causal = position[None, :] <= position[:, None]
    scores = (
        jnp.einsum("btgrh,bugh->bgrtu", query_heads, key_heads, preferred_element_type=jnp.float32)
        * score_scale
    )
    scores = jnp.where(causal, scores, -1e30)
    row_max = jnp.max(scores, axis=-1, keepdims=True)
    exp_scores = jnp.exp(scores - row_max)
    softmax_out = exp_scores / jnp.sum(exp_scores, axis=-1, keepdims=True)
    softmax_low = softmax_out.astype(jnp.bfloat16)
    context = jnp.einsum(
        "bgrtu,bugh->btgrh", softmax_low, value_heads, preferred_element_type=jnp.float32
    ).astype(jnp.bfloat16)
    return (softmax_out, softmax_low, context)


def attention_backward(grad_context, query_heads, key_heads, value_heads, softmax_out, softmax_low):
    score_scale = query_heads.shape[-1] ** (-0.5)
    grad_soft = jnp.einsum(
        "btgrh,bugh->bgrtu", grad_context, value_heads, preferred_element_type=jnp.float32
    )
    row_inner = jnp.sum(grad_soft * softmax_out, axis=-1, keepdims=True)
    grad_scores = (softmax_out * (grad_soft - row_inner) * score_scale).astype(jnp.bfloat16)
    grad_query = jnp.einsum(
        "bgrtu,bugh->btgrh", grad_scores, key_heads, preferred_element_type=jnp.float32
    ).astype(jnp.bfloat16)
    grad_key = jnp.einsum(
        "bgrtu,btgrh->bugh", grad_scores, query_heads, preferred_element_type=jnp.float32
    ).astype(jnp.bfloat16)
    grad_value = jnp.einsum(
        "bgrtu,btgrh->bugh", softmax_low, grad_context, preferred_element_type=jnp.float32
    ).astype(jnp.bfloat16)
    return (grad_query, grad_key, grad_value)


def on_device(tokens, grad_out, counts, gain, wq, wk, wv, wo):
    groups = lax.axis_size("tensor")
    dp_size = lax.axis_size("dp")
    replica = lax.axis_index("dp")
    own_count = counts[replica]
    blocks, length, shard_width = tokens.shape
    full_width = shard_width * groups
    d_local = gain.shape[0]
    q_cols = wq.shape[1]
    k_cols = wk.shape[1]
    o_rows = wo.shape[0]
    c1 = q_cols
    c2 = c1 + k_cols
    c3 = c2 + k_cols
    c4 = c3 + o_rows
    pack = jnp.concatenate(
        [wq, wk, wv, wo.T, jnp.pad(gain.reshape(d_local, 1), ((0, 0), (0, 127)))], axis=1
    )
    packed = lax.all_gather(pack, "dp", axis=0, tiled=True)
    width = packed.shape[1]
    gain_all = packed[:, c4]
    half = dp_size // 2
    pair = [(i, (i + half) % dp_size) for i in range(dp_size)]
    partner_count = counts[(replica + half) % dp_size]
    lent = lax.ppermute(jnp.stack([tokens[1], grad_out[1]]), "dp", pair)
    borrow = own_count == 0
    work_live = jnp.where(borrow, partner_count >= 2, own_count >= 1)
    live_mask = work_live.astype(jnp.bfloat16)
    work_tokens = jnp.where(borrow, lent[0], tokens[0])
    work_grad = jnp.where(borrow, lent[1], grad_out[0]) * live_mask
    piece = jnp.stack([work_tokens, work_grad])
    spread = jnp.broadcast_to(piece[None], (groups,) + piece.shape)
    gathered = lax.all_to_all(spread, "tensor", 0, 0, tiled=True)
    both = jnp.moveaxis(gathered, 0, 2).reshape(2, length, full_width)
    wide_in, upstream = both[0], both[1]
    repeat = HEADS // KV
    kv_local = k_cols // HD
    wide_float = wide_in.astype(jnp.float32)
    inverse_rms = lax.rsqrt(jnp.mean(wide_float * wide_float, axis=-1, keepdims=True) + epsilon)
    unit_rows = wide_float * inverse_rms
    gain_float = gain_all.astype(jnp.float32)
    normed_float = unit_rows * gain_float
    normed = normed_float.astype(jnp.bfloat16)
    lhs = jnp.concatenate([normed, upstream], axis=0)
    proj = jnp.einsum("td,dk->tk", lhs, packed, preferred_element_type=jnp.float32).astype(
        jnp.bfloat16
    )
    qkv = proj[:length]
    query_heads = qkv[:, :c1].reshape(1, length, kv_local, repeat, HD)
    key_heads = qkv[:, c1:c2].reshape(1, length, kv_local, HD)
    value_heads = qkv[:, c2:c3].reshape(1, length, kv_local, HD)
    softmax_out, softmax_low, context = attention_forward(query_heads, key_heads, value_heads)
    context_flat = context.reshape(length, kv_local * repeat * HD)
    context_wide = jnp.pad(context_flat, ((0, 0), (c3, width - c4)))
    upstream_blk = upstream.reshape(length, dp_size, d_local)
    grad_context = proj[length:, c3:c4]
    grad_query, grad_key, grad_value = attention_backward(
        grad_context.reshape(1, length, kv_local, repeat, HD),
        query_heads,
        key_heads,
        value_heads,
        softmax_out,
        softmax_low,
    )
    grad_qkv = jnp.concatenate(
        [
            grad_query.reshape(length, c1),
            grad_key.reshape(length, k_cols),
            grad_value.reshape(length, k_cols),
        ],
        axis=1,
    )
    grad_wide = jnp.pad(grad_qkv, ((0, 0), (0, width - c3)))
    back = jnp.einsum(
        "tk,dk->td",
        jnp.concatenate([context_wide, grad_wide], axis=0),
        packed,
        preferred_element_type=jnp.float32,
    )
    partial_value = back[:length]
    normed_terms = back[length:]
    grad_w_qkv = jnp.einsum(
        "tjl,tk->jlk", normed.reshape(length, dp_size, d_local), grad_qkv,
        preferred_element_type=jnp.float32,
    )
    grad_output_t = jnp.einsum(
        "tjl,tk->jlk", upstream_blk, context_flat, preferred_element_type=jnp.float32
    )
    term_low = normed_terms.astype(jnp.bfloat16)
    term_float = term_low.astype(jnp.float32)
    row_dot = jnp.sum(term_float * normed_float, axis=-1)
    gain_part = jnp.sum(term_float * unit_rows, axis=0)
    extra = jnp.pad(row_dot, (0, shard_width - length)).reshape(1, shard_width)
    extra = jnp.pad(extra, ((0, 15), (0, 0))).astype(jnp.bfloat16)

    def by_chunk(x):
        return x.reshape(length, groups, shard_width).transpose(1, 0, 2)

    payload = jnp.concatenate(
        [
            by_chunk(partial_value.astype(jnp.bfloat16)),
            by_chunk(term_low),
            jnp.broadcast_to(extra[None], (groups,) + extra.shape),
        ],
        axis=1,
    )
    received = lax.all_to_all(payload, "tensor", 0, 0, tiled=True)
    reduced = jnp.sum(received.astype(jnp.float32), axis=0)
    attn_sum = reduced[:length]
    grad_normed = reduced[length : 2 * length]
    row_mean = (reduced[2 * length, :length] / full_width)[:, None]
    work_mixed = ((work_tokens.astype(jnp.float32) + attn_sum) * live_mask.astype(jnp.float32)).astype(
        jnp.bfloat16
    )
    shard_start = lax.axis_index("tensor") * shard_width
    own_unit = lax.dynamic_slice_in_dim(unit_rows, shard_start, shard_width, 1)
    own_gain = lax.dynamic_slice_in_dim(gain_float, shard_start, shard_width, 0)
    own_grad = inverse_rms * (grad_normed * own_gain - own_unit * row_mean)
    work_grad_tokens = (work_grad.astype(jnp.float32) + own_grad).astype(jnp.bfloat16)
    work_out = jnp.stack([work_mixed, work_grad_tokens])
    returned = lax.ppermute(work_out, "dp", pair)
    first = jnp.where(own_count >= 1, work_out, jnp.zeros_like(work_out))
    second = jnp.where(own_count >= 2, returned, jnp.zeros_like(returned))
    mixed_block = jnp.stack([first[0], second[0]])
    grad_block = jnp.stack([first[1], second[1]])
    gpack = jnp.concatenate(
        [
            grad_w_qkv.astype(jnp.bfloat16),
            grad_output_t.astype(jnp.bfloat16),
            jnp.pad(gain_part.reshape(dp_size, d_local, 1), ((0, 0), (0, 0), (0, 127))).astype(
                jnp.bfloat16
            ),
        ],
        axis=2,
    )
    greduced = lax.psum_scatter(gpack, "dp", scatter_dimension=0, tiled=True)[0].astype(jnp.float32)
    grad_wq = greduced[:, :c1]
    grad_wk = greduced[:, c1:c2]
    grad_wv = greduced[:, c2:c3]
    grad_wo = greduced[:, c3:c4].T
    gain_spread = jnp.broadcast_to(greduced[:, c4][None], (groups, d_local))
    grad_gain = jnp.sum(lax.all_to_all(gain_spread, "tensor", 0, 0, tiled=True), axis=0)
    return (mixed_block, grad_block, grad_gain, grad_wq, grad_wk, grad_wv, grad_wo)


def solution(mesh):
    return jax.shard_map(
        on_device,
        mesh=mesh,
        in_specs=(
            P("dp", None, "tensor"),
            P("dp", None, "tensor"),
            P(),
            P("dp"),
            P("dp", "tensor"),
            P("dp", "tensor"),
            P("dp", "tensor"),
            P("tensor", "dp"),
        ),
        out_specs=(
            P("dp", None, "tensor"),
            P("dp", None, "tensor"),
            P("dp"),
            P("dp", "tensor"),
            P("dp", "tensor"),
            P("dp", "tensor"),
            P("tensor", "dp"),
        ),
        check_vma=False,
    )
```

```python
import jax
import jax.numpy as jnp
from jax import lax
from jax.sharding import PartitionSpec as P

HEADS = 32
KV = 8
HD = 128


epsilon = 1e-05


def attention_forward(query_heads, key_heads, value_heads):
    length = query_heads.shape[1]
    score_scale = query_heads.shape[-1] ** (-0.5)
    position = jnp.arange(length)
    causal = position[None, :] <= position[:, None]
    scores = (
        jnp.einsum("btgrh,bugh->bgrtu", query_heads, key_heads, preferred_element_type=jnp.float32)
        * score_scale
    )
    scores = jnp.where(causal, scores, -1e30)
    row_max = jnp.max(scores, axis=-1, keepdims=True)
    exp_scores = jnp.exp(scores - row_max)
    softmax_out = exp_scores / jnp.sum(exp_scores, axis=-1, keepdims=True)
    softmax_low = softmax_out.astype(jnp.bfloat16)
    context = jnp.einsum(
        "bgrtu,bugh->btgrh", softmax_low, value_heads, preferred_element_type=jnp.float32
    ).astype(jnp.bfloat16)
    return (softmax_out, softmax_low, context)


def attention_backward(grad_context, query_heads, key_heads, value_heads, softmax_out, softmax_low):
    score_scale = query_heads.shape[-1] ** (-0.5)
    grad_soft = jnp.einsum(
        "btgrh,bugh->bgrtu", grad_context, value_heads, preferred_element_type=jnp.float32
    )
    row_inner = jnp.sum(grad_soft * softmax_out, axis=-1, keepdims=True)
    grad_scores = (softmax_out * (grad_soft - row_inner) * score_scale).astype(jnp.bfloat16)
    grad_query = jnp.einsum(
        "bgrtu,bugh->btgrh", grad_scores, key_heads, preferred_element_type=jnp.float32
    ).astype(jnp.bfloat16)
    grad_key = jnp.einsum(
        "bgrtu,btgrh->bugh", grad_scores, query_heads, preferred_element_type=jnp.float32
    ).astype(jnp.bfloat16)
    grad_value = jnp.einsum(
        "bgrtu,btgrh->bugh", softmax_low, grad_context, preferred_element_type=jnp.float32
    ).astype(jnp.bfloat16)
    return (grad_query, grad_key, grad_value)


def on_device(tokens, grad_out, counts, gain, wq, wk, wv, wo):
    groups = lax.axis_size("tensor")
    dp_size = lax.axis_size("dp")
    replica = lax.axis_index("dp")
    own_count = counts[replica]
    blocks, length, shard_width = tokens.shape
    full_width = shard_width * groups
    d_local = gain.shape[0]
    q_cols = wq.shape[1]
    k_cols = wk.shape[1]
    o_rows = wo.shape[0]
    c1 = q_cols
    c2 = c1 + k_cols
    c3 = c2 + k_cols
    c4 = c3 + o_rows
    pack = jnp.concatenate([wq, wk, wv, wo.T], axis=1)
    packed = lax.all_gather(pack, "dp", axis=0, tiled=True)
    width = packed.shape[1]
    gain_spread = jnp.broadcast_to(gain[None], (dp_size, d_local))
    gain_all = lax.all_to_all(gain_spread, "dp", 0, 0, tiled=True).reshape(full_width)
    half = dp_size // 2
    pair = [(i, (i + half) % dp_size) for i in range(dp_size)]
    partner_count = counts[(replica + half) % dp_size]
    lent = lax.ppermute(jnp.stack([tokens[1], grad_out[1]]), "dp", pair)
    borrow = own_count == 0
    work_live = jnp.where(borrow, partner_count >= 2, own_count >= 1)
    live_mask = work_live.astype(jnp.bfloat16)
    work_tokens = jnp.where(borrow, lent[0], tokens[0])
    work_grad = jnp.where(borrow, lent[1], grad_out[0]) * live_mask
    piece = jnp.stack([work_tokens, work_grad])
    spread = jnp.broadcast_to(piece[None], (groups,) + piece.shape)
    gathered = lax.all_to_all(spread, "tensor", 0, 0, tiled=True)
    both = jnp.moveaxis(gathered, 0, 2).reshape(2, length, full_width)
    wide_in, upstream = both[0], both[1]
    repeat = HEADS // KV
    kv_local = k_cols // HD
    wide_float = wide_in.astype(jnp.float32)
    inverse_rms = lax.rsqrt(jnp.mean(wide_float * wide_float, axis=-1, keepdims=True) + epsilon)
    unit_rows = wide_float * inverse_rms
    gain_float = gain_all.astype(jnp.float32)
    normed_float = unit_rows * gain_float
    normed = normed_float.astype(jnp.bfloat16)
    lhs = jnp.concatenate([normed, upstream], axis=0)
    proj = jnp.einsum("td,dk->tk", lhs, packed, preferred_element_type=jnp.float32).astype(
        jnp.bfloat16
    )
    qkv = proj[:length]
    query_heads = qkv[:, :c1].reshape(1, length, kv_local, repeat, HD)
    key_heads = qkv[:, c1:c2].reshape(1, length, kv_local, HD)
    value_heads = qkv[:, c2:c3].reshape(1, length, kv_local, HD)
    softmax_out, softmax_low, context = attention_forward(query_heads, key_heads, value_heads)
    context_flat = context.reshape(length, kv_local * repeat * HD)
    context_wide = jnp.pad(context_flat, ((0, 0), (c3, width - c4)))
    upstream_blk = upstream.reshape(length, dp_size, d_local)
    grad_context = proj[length:, c3:c4]
    grad_query, grad_key, grad_value = attention_backward(
        grad_context.reshape(1, length, kv_local, repeat, HD),
        query_heads,
        key_heads,
        value_heads,
        softmax_out,
        softmax_low,
    )
    grad_qkv = jnp.concatenate(
        [
            grad_query.reshape(length, c1),
            grad_key.reshape(length, k_cols),
            grad_value.reshape(length, k_cols),
        ],
        axis=1,
    )
    grad_wide = jnp.pad(grad_qkv, ((0, 0), (0, width - c3)))
    back = jnp.einsum(
        "tk,dk->td",
        jnp.concatenate([context_wide, grad_wide], axis=0),
        packed,
        preferred_element_type=jnp.float32,
    )
    partial_value = back[:length]
    normed_terms = back[length:]
    grad_w_qkv = jnp.einsum(
        "tjl,tk->jlk", normed.reshape(length, dp_size, d_local), grad_qkv,
        preferred_element_type=jnp.float32,
    )
    grad_output_t = jnp.einsum(
        "tjl,tk->jlk", upstream_blk, context_flat, preferred_element_type=jnp.float32
    )
    term_low = normed_terms.astype(jnp.bfloat16)
    term_float = term_low.astype(jnp.float32)
    row_dot = jnp.sum(term_float * normed_float, axis=-1)
    gain_part = jnp.sum(term_float * unit_rows, axis=0)
    extra = jnp.pad(row_dot, (0, shard_width - length)).reshape(1, shard_width)
    extra = jnp.pad(extra, ((0, 15), (0, 0))).astype(jnp.bfloat16)

    def by_chunk(x):
        return x.reshape(length, groups, shard_width).transpose(1, 0, 2)

    payload = jnp.concatenate(
        [
            by_chunk(partial_value.astype(jnp.bfloat16)),
            by_chunk(term_low),
            jnp.broadcast_to(extra[None], (groups,) + extra.shape),
        ],
        axis=1,
    )
    received = lax.all_to_all(payload, "tensor", 0, 0, tiled=True)
    reduced = jnp.sum(received.astype(jnp.float32), axis=0)
    attn_sum = reduced[:length]
    grad_normed = reduced[length : 2 * length]
    row_mean = (reduced[2 * length, :length] / full_width)[:, None]
    work_mixed = ((work_tokens.astype(jnp.float32) + attn_sum) * live_mask.astype(jnp.float32)).astype(
        jnp.bfloat16
    )
    shard_start = lax.axis_index("tensor") * shard_width
    own_unit = lax.dynamic_slice_in_dim(unit_rows, shard_start, shard_width, 1)
    own_gain = lax.dynamic_slice_in_dim(gain_float, shard_start, shard_width, 0)
    own_grad = inverse_rms * (grad_normed * own_gain - own_unit * row_mean)
    work_grad_tokens = (work_grad.astype(jnp.float32) + own_grad).astype(jnp.bfloat16)
    work_out = jnp.stack([work_mixed, work_grad_tokens])
    returned = lax.ppermute(work_out, "dp", pair)
    first = jnp.where(own_count >= 1, work_out, jnp.zeros_like(work_out))
    second = jnp.where(own_count >= 2, returned, jnp.zeros_like(returned))
    mixed_block = jnp.stack([first[0], second[0]])
    grad_block = jnp.stack([first[1], second[1]])
    gpack = jnp.concatenate(
        [
            grad_w_qkv.astype(jnp.bfloat16),
            grad_output_t.astype(jnp.bfloat16),
        ],
        axis=2,
    )
    greduced = lax.psum_scatter(gpack, "dp", scatter_dimension=0, tiled=True)[0].astype(jnp.float32)
    grad_wq = greduced[:, :c1]
    grad_wk = greduced[:, c1:c2]
    grad_wv = greduced[:, c2:c3]
    grad_wo = greduced[:, c3:c4].T
    gain_replicas = lax.all_to_all(gain_part.reshape(dp_size, d_local), "dp", 0, 0, tiled=True)
    gain_groups = jnp.broadcast_to(jnp.sum(gain_replicas, axis=0)[None], (groups, d_local))
    grad_gain = jnp.sum(lax.all_to_all(gain_groups, "tensor", 0, 0, tiled=True), axis=0)
    return (mixed_block, grad_block, grad_gain, grad_wq, grad_wk, grad_wv, grad_wo)


def solution(mesh):
    return jax.shard_map(
        on_device,
        mesh=mesh,
        in_specs=(
            P("dp", None, "tensor"),
            P("dp", None, "tensor"),
            P(),
            P("dp"),
            P("dp", "tensor"),
            P("dp", "tensor"),
            P("dp", "tensor"),
            P("tensor", "dp"),
        ),
        out_specs=(
            P("dp", None, "tensor"),
            P("dp", None, "tensor"),
            P("dp"),
            P("dp", "tensor"),
            P("dp", "tensor"),
            P("dp", "tensor"),
            P("tensor", "dp"),
        ),
        check_vma=False,
    )
```

```python
import jax
import jax.numpy as jnp
from jax import lax
from jax.sharding import PartitionSpec as P

HEADS = 32
KV = 8
HD = 128


epsilon = 1e-05


def attention_forward(query_heads, key_heads, value_heads):
    length = query_heads.shape[1]
    score_scale = query_heads.shape[-1] ** (-0.5)
    position = jnp.arange(length)
    causal = position[None, :] <= position[:, None]
    scores = (
        jnp.einsum("btgrh,bugh->bgrtu", query_heads, key_heads, preferred_element_type=jnp.float32)
        * score_scale
    )
    scores = jnp.where(causal, scores, -1e30)
    row_max = jnp.max(scores, axis=-1, keepdims=True)
    exp_scores = jnp.exp(scores - row_max)
    softmax_out = exp_scores / jnp.sum(exp_scores, axis=-1, keepdims=True)
    softmax_low = softmax_out.astype(jnp.bfloat16)
    context = jnp.einsum(
        "bgrtu,bugh->btgrh", softmax_low, value_heads, preferred_element_type=jnp.float32
    ).astype(jnp.bfloat16)
    return (softmax_out, softmax_low, context)


def attention_backward(grad_context, query_heads, key_heads, value_heads, softmax_out, softmax_low):
    score_scale = query_heads.shape[-1] ** (-0.5)
    grad_soft = jnp.einsum(
        "btgrh,bugh->bgrtu", grad_context, value_heads, preferred_element_type=jnp.float32
    )
    row_inner = jnp.sum(grad_soft * softmax_out, axis=-1, keepdims=True)
    grad_scores = (softmax_out * (grad_soft - row_inner) * score_scale).astype(jnp.bfloat16)
    grad_query = jnp.einsum(
        "bgrtu,bugh->btgrh", grad_scores, key_heads, preferred_element_type=jnp.float32
    ).astype(jnp.bfloat16)
    grad_key = jnp.einsum(
        "bgrtu,btgrh->bugh", grad_scores, query_heads, preferred_element_type=jnp.float32
    ).astype(jnp.bfloat16)
    grad_value = jnp.einsum(
        "bgrtu,btgrh->bugh", softmax_low, grad_context, preferred_element_type=jnp.float32
    ).astype(jnp.bfloat16)
    return (grad_query, grad_key, grad_value)


def on_device(tokens, grad_out, counts, gain, wq, wk, wv, wo):
    groups = lax.axis_size("tensor")
    dp_size = lax.axis_size("dp")
    replica = lax.axis_index("dp")
    own_count = counts[replica]
    blocks, length, shard_width = tokens.shape
    full_width = shard_width * groups
    d_local = gain.shape[0]
    q_cols = wq.shape[1]
    k_cols = wk.shape[1]
    o_rows = wo.shape[0]
    c1 = q_cols
    c2 = c1 + k_cols
    c3 = c2 + k_cols
    c4 = c3 + o_rows
    pack = jnp.concatenate([wq, wk, wv], axis=1)
    packed = lax.all_gather(pack, "dp", axis=0, tiled=True)
    width = packed.shape[1]
    wo_spread = jnp.broadcast_to(wo.T[None], (dp_size,) + wo.T.shape)
    wo_blk = lax.all_to_all(wo_spread, "dp", 0, 0, tiled=True)
    gain_spread = jnp.broadcast_to(gain[None], (dp_size, d_local))
    gain_all = lax.all_to_all(gain_spread, "dp", 0, 0, tiled=True).reshape(full_width)
    half = dp_size // 2
    pair = [(i, (i + half) % dp_size) for i in range(dp_size)]
    partner_count = counts[(replica + half) % dp_size]
    lent = lax.ppermute(jnp.stack([tokens[1], grad_out[1]]), "dp", pair)
    borrow = own_count == 0
    work_live = jnp.where(borrow, partner_count >= 2, own_count >= 1)
    live_mask = work_live.astype(jnp.bfloat16)
    work_tokens = jnp.where(borrow, lent[0], tokens[0])
    work_grad = jnp.where(borrow, lent[1], grad_out[0]) * live_mask
    piece = jnp.stack([work_tokens, work_grad])
    spread = jnp.broadcast_to(piece[None], (groups,) + piece.shape)
    gathered = lax.all_to_all(spread, "tensor", 0, 0, tiled=True)
    both = jnp.moveaxis(gathered, 0, 2).reshape(2, length, full_width)
    wide_in, upstream = both[0], both[1]
    repeat = HEADS // KV
    kv_local = k_cols // HD
    wide_float = wide_in.astype(jnp.float32)
    inverse_rms = lax.rsqrt(jnp.mean(wide_float * wide_float, axis=-1, keepdims=True) + epsilon)
    unit_rows = wide_float * inverse_rms
    gain_float = gain_all.astype(jnp.float32)
    normed_float = unit_rows * gain_float
    normed = normed_float.astype(jnp.bfloat16)
    qkv = jnp.einsum("td,dk->tk", normed, packed, preferred_element_type=jnp.float32).astype(
        jnp.bfloat16
    )
    query_heads = qkv[:, :c1].reshape(1, length, kv_local, repeat, HD)
    key_heads = qkv[:, c1:c2].reshape(1, length, kv_local, HD)
    value_heads = qkv[:, c2:c3].reshape(1, length, kv_local, HD)
    softmax_out, softmax_low, context = attention_forward(query_heads, key_heads, value_heads)
    context_flat = context.reshape(length, kv_local * repeat * HD)
    upstream_blk = upstream.reshape(length, dp_size, d_local)
    grad_context = jnp.einsum(
        "tjl,jlk->tk", upstream_blk, wo_blk, preferred_element_type=jnp.float32
    ).astype(jnp.bfloat16)
    grad_query, grad_key, grad_value = attention_backward(
        grad_context.reshape(1, length, kv_local, repeat, HD),
        query_heads,
        key_heads,
        value_heads,
        softmax_out,
        softmax_low,
    )
    grad_qkv = jnp.concatenate(
        [
            grad_query.reshape(length, c1),
            grad_key.reshape(length, k_cols),
            grad_value.reshape(length, k_cols),
        ],
        axis=1,
    )
    normed_terms = jnp.einsum("tk,dk->td", grad_qkv, packed, preferred_element_type=jnp.float32)
    partial_value = jnp.einsum(
        "tk,jlk->tjl", context_flat, wo_blk, preferred_element_type=jnp.float32
    ).reshape(length, full_width)
    grad_w_qkv = jnp.einsum(
        "tjl,tk->jlk", normed.reshape(length, dp_size, d_local), grad_qkv,
        preferred_element_type=jnp.float32,
    )
    grad_output_t = jnp.einsum(
        "tjl,tk->jlk", upstream_blk, context_flat, preferred_element_type=jnp.float32
    )
    term_low = normed_terms.astype(jnp.bfloat16)
    term_float = term_low.astype(jnp.float32)
    row_dot = jnp.sum(term_float * normed_float, axis=-1)
    gain_part = jnp.sum(term_float * unit_rows, axis=0)
    extra = jnp.pad(row_dot, (0, shard_width - length)).reshape(1, shard_width)
    extra = jnp.pad(extra, ((0, 15), (0, 0))).astype(jnp.bfloat16)

    def by_chunk(x):
        return x.reshape(length, groups, shard_width).transpose(1, 0, 2)

    payload = jnp.concatenate(
        [
            by_chunk(partial_value.astype(jnp.bfloat16)),
            by_chunk(term_low),
            jnp.broadcast_to(extra[None], (groups,) + extra.shape),
        ],
        axis=1,
    )
    received = lax.all_to_all(payload, "tensor", 0, 0, tiled=True)
    reduced = jnp.sum(received.astype(jnp.float32), axis=0)
    attn_sum = reduced[:length]
    grad_normed = reduced[length : 2 * length]
    row_mean = (reduced[2 * length, :length] / full_width)[:, None]
    work_mixed = ((work_tokens.astype(jnp.float32) + attn_sum) * live_mask.astype(jnp.float32)).astype(
        jnp.bfloat16
    )
    shard_start = lax.axis_index("tensor") * shard_width
    own_unit = lax.dynamic_slice_in_dim(unit_rows, shard_start, shard_width, 1)
    own_gain = lax.dynamic_slice_in_dim(gain_float, shard_start, shard_width, 0)
    own_grad = inverse_rms * (grad_normed * own_gain - own_unit * row_mean)
    work_grad_tokens = (work_grad.astype(jnp.float32) + own_grad).astype(jnp.bfloat16)
    work_out = jnp.stack([work_mixed, work_grad_tokens])
    returned = lax.ppermute(work_out, "dp", pair)
    first = jnp.where(own_count >= 1, work_out, jnp.zeros_like(work_out))
    second = jnp.where(own_count >= 2, returned, jnp.zeros_like(returned))
    mixed_block = jnp.stack([first[0], second[0]])
    grad_block = jnp.stack([first[1], second[1]])
    gpack = jnp.concatenate(
        [
            grad_w_qkv.astype(jnp.bfloat16),
            grad_output_t.astype(jnp.bfloat16),
        ],
        axis=2,
    )
    greduced = lax.psum_scatter(gpack, "dp", scatter_dimension=0, tiled=True)[0].astype(jnp.float32)
    grad_wq = greduced[:, :c1]
    grad_wk = greduced[:, c1:c2]
    grad_wv = greduced[:, c2:c3]
    grad_wo = greduced[:, c3:c4].T
    gain_replicas = lax.all_to_all(gain_part.reshape(dp_size, d_local), "dp", 0, 0, tiled=True)
    gain_groups = jnp.broadcast_to(jnp.sum(gain_replicas, axis=0)[None], (groups, d_local))
    grad_gain = jnp.sum(lax.all_to_all(gain_groups, "tensor", 0, 0, tiled=True), axis=0)
    return (mixed_block, grad_block, grad_gain, grad_wq, grad_wk, grad_wv, grad_wo)


def solution(mesh):
    return jax.shard_map(
        on_device,
        mesh=mesh,
        in_specs=(
            P("dp", None, "tensor"),
            P("dp", None, "tensor"),
            P(),
            P("dp"),
            P("dp", "tensor"),
            P("dp", "tensor"),
            P("dp", "tensor"),
            P("tensor", "dp"),
        ),
        out_specs=(
            P("dp", None, "tensor"),
            P("dp", None, "tensor"),
            P("dp"),
            P("dp", "tensor"),
            P("dp", "tensor"),
            P("dp", "tensor"),
            P("tensor", "dp"),
        ),
        check_vma=False,
    )
```
